768 devices in a mesh: dp: 64 (over x, y, core), seq: 12 (over z).
Axes of the slice: x: 4, y: 8, z: 12, core: 2. Of those that a mesh axis runs over, the one named last changes fastest.
Arguments:
- audio_blocks: bfloat16 [64, 1536, 40], P('dp', 'seq'), may hold values from -6 to 6
- send_list: int32 [12, 64, 256], P('seq', 'dp'), may hold values from -1 to 127, as said below
- place_list: int32 [12, 64, 128], P('seq', 'dp'), may hold values from 0 to 255, as said below
- cotangent: bfloat16 [64, 6144, 512], P('dp', 'seq'), may hold values from -0.009765625 to 0.009765625
- conv_zero: bfloat16 [10, 512], replicated, may hold values from -2 to 2
- conv_one: bfloat16 [1536, 512], replicated, may hold values from -0.15625 to 0.15625
- gain_zero: float32 [512], replicated, may hold values from 0.25 to 1.75
- bias_zero: float32 [512], replicated, may hold values from -3 to 3
- gain_one: float32 [512], replicated, may hold values from 0.25 to 1.75
- bias_one: float32 [512], replicated, may hold values from -3 to 3
Outputs:
- features: bfloat16 [64, 6144, 512], P('dp', 'seq')
- grad_conv_one: float32 [1536, 512], P('dp')
- grad_conv_zero: float32 [10, 512], replicated
- grad_gain_zero: float32 [512], replicated
- grad_bias_zero: float32 [512], replicated
- grad_gain_one: float32 [512], replicated
- grad_bias_one: float32 [512], replicated
The draws below stay inside these ranges and needn't reach their ends.
Inputs may be any that keep to these rules, and one draw needn't show every extreme that they name: `send_list`: row (s, i) holds, in 4 slots for each destination device in order, the local blocks of store s on device i sent there; -1 marks an empty slot. Each of the 128 blocks appears exactly once in its row, and in every store some source fills all 4 slots to some destination. `place_list`: row (s, j) names 128 distinct filled received slots (source times 4 plus slot) for device j and store s, in the order of its segment.
All inputs are finite; a program needn't handle non-finite values.
Results may differ from the reference program's by a relative error of at most 0.0057.
Values may be sent and summed in bfloat16 or wider, within the bound.
A program may use at most 64 MiB of HBM per device.

```python
import jax
import jax.numpy as jnp
from jax import lax

C = 512
FR1 = 512
CAP = 4
ROWS = 128
BLEN = 40
N_DP = 64
N_SEQ = 12


def store_lists(key):
    subkeys = jax.random.split(key, 5)
    half_count = N_DP // 2
    tilted = jax.random.randint(subkeys[0], (half_count, half_count), -2, 3)
    tilted = tilted.at[0, 0].set(2)
    upper_half = jnp.stack([2 + tilted, 2 - tilted], axis=-1)
    lower_half = jnp.stack([2 - tilted, 2 + tilted], axis=-1)
    counts = jnp.stack([upper_half, lower_half], axis=1).reshape(N_DP, N_DP)
    counts = counts[jax.random.permutation(subkeys[1], N_DP)][:, jax.random.permutation(subkeys[2], N_DP)]
    orders = jax.vmap(lambda subkey: jax.random.permutation(subkey, ROWS))(jax.random.split(subkeys[3], N_DP))
    starts = jnp.cumsum(counts, axis=1) - counts
    slot_ids = jnp.arange(CAP)
    wanted = starts[:, :, None] + slot_ids
    filled = slot_ids < counts[:, :, None]
    local_ids = jnp.take_along_axis(orders, jnp.clip(wanted, 0, ROWS - 1).reshape(N_DP, N_DP * CAP), axis=1)
    send_lists = jnp.where(filled.reshape(N_DP, N_DP * CAP), local_ids, -1)
    arrived = jnp.transpose(filled, (1, 0, 2)).reshape(N_DP, N_DP * CAP)
    rank_ids = jax.vmap(lambda subkey: jax.random.permutation(subkey, N_DP * CAP))(jax.random.split(subkeys[4], N_DP))
    scores = jnp.where(arrived, rank_ids, rank_ids + N_DP * CAP)
    places = jnp.argsort(scores, axis=1)[:, :ROWS]
    return (send_lists.astype(jnp.int32), places.astype(jnp.int32))


def reassign_lists(key):
    base_key = jax.random.fold_in(key, 31)
    return jax.vmap(store_lists)(jax.random.split(base_key, N_SEQ))


def draw_send_list(key, part):
    return reassign_lists(key)[0]


def draw_place_list(key, part):
    return reassign_lists(key)[1]


def steps_of(key, dims, cuts, smallest, top_value):
    def one(position, blocks):
        steps = jax.random.uniform(jax.random.fold_in(jax.random.fold_in(key, 6), position), (blocks,), jnp.float32, smallest / len(cuts), top_value / len(cuts))
        return jnp.repeat(jnp.exp(steps), dims[position] // blocks).reshape((-1,) + (1,) * (len(dims) - position - 1))

    loudness = one(*cuts[0])
    for cut in cuts[1:]:
        loudness = loudness * one(*cut)
    return loudness


def scatter_about(rng, shape, scale, reach, cuts=(), held_as=jnp.bfloat16):
    values = scale * jax.random.normal(rng, shape, jnp.float32)
    if cuts:
        values = values * steps_of(rng, shape, cuts, -0.22, 0.18)
    return jnp.clip(values, -reach, reach).astype(held_as)


def setup_inputs(seed: int = 0) -> dict:
    streams_of = jax.random.split(jax.random.key(seed), 11)
    return {
        "audio_blocks": scatter_about(streams_of[0], (N_DP, N_SEQ * ROWS, BLEN), 1.0, 6.0, ((0, 64), (1, 12))),
        "send_list": draw_send_list(jax.random.fold_in(streams_of[10], 71), 0),
        "place_list": draw_place_list(jax.random.fold_in(streams_of[10], 71), 0),
        "cotangent": scatter_about(streams_of[3], (N_DP, N_SEQ * FR1, C), (N_DP * N_SEQ * FR1) ** -0.5, 0.009765625, ((0, 64), (1, 12))),
        "conv_zero": scatter_about(streams_of[4], (10, C), 10 ** -0.5, 2.0),
        "conv_one": scatter_about(streams_of[5], (3 * C, C), (3 * C) ** -0.5, 0.15625),
        "gain_zero": jnp.clip(1.0 + 0.15 * jax.random.normal(streams_of[6], (C,), jnp.float32), 0.25, 1.75),
        "bias_zero": scatter_about(streams_of[7], (C,), 0.5, 3.0, (), jnp.float32),
        "gain_one": jnp.clip(1.0 + 0.15 * jax.random.normal(streams_of[8], (C,), jnp.float32), 0.25, 1.75),
        "bias_one": scatter_about(streams_of[9], (C,), 0.5, 3.0, (), jnp.float32),
    }


norm_eps = 1e-05

def gelu_slope(argument):
    return 0.5 * (1.0 + lax.erf(argument * 0.7071067811865476)) + argument * jnp.exp(-0.5 * argument * argument) * 0.3989422804014327

def norm_forward(pre_act, gain_vec, bias_vec):
    center = pre_act - lax.optimization_barrier(jnp.mean(pre_act, axis=-1, keepdims=True))
    spread = lax.rsqrt(lax.optimization_barrier(jnp.mean(center * center, axis=-1, keepdims=True)) + norm_eps)
    scaled = center * spread
    normed = scaled * gain_vec + bias_vec
    return (jax.nn.gelu(normed, approximate=False), scaled, spread, normed)

def norm_backward(upstream, gain_vec, scaled, spread, normed):
    inner_grad = upstream * gelu_slope(normed)
    grad_gain = lax.optimization_barrier(jnp.sum(inner_grad * scaled, axis=0))
    grad_bias = lax.optimization_barrier(jnp.sum(inner_grad, axis=0))
    pushed = inner_grad * gain_vec
    back_grad = spread * (pushed - lax.optimization_barrier(jnp.mean(pushed, axis=-1, keepdims=True)) - scaled * lax.optimization_barrier(jnp.mean(pushed * scaled, axis=-1, keepdims=True)))
    return (back_grad, grad_gain, grad_bias)

def frame_patches(samples, frames):
    sample_rows = samples[:5 * (frames + 1)].reshape(frames + 1, 5)
    return jnp.concatenate([sample_rows[:-1], sample_rows[1:]], axis=1)

def layer_one(frames_in, frames_one, conv_one, gain_one, bias_one, upstream):
    width = conv_one.shape[1]
    frame_pairs = frames_in[:2 * frames_one].reshape(frames_one, 2, width)
    first_tap = frame_pairs[:, 0]
    second_tap = frame_pairs[:, 1]
    third_tap = jnp.concatenate([first_tap[1:], frames_in[2 * frames_one:]], axis=0)
    pre_one = jnp.dot(first_tap, conv_one[:width], preferred_element_type=jnp.float32) + jnp.dot(second_tap, conv_one[width:2 * width], preferred_element_type=jnp.float32) + jnp.dot(third_tap, conv_one[2 * width:], preferred_element_type=jnp.float32)
    act_one, scaled_one, spread_one, normed_one = norm_forward(pre_one, gain_one, bias_one)
    back_one, grad_gain_one, grad_bias_one = norm_backward(upstream.astype(jnp.float32), gain_one, scaled_one, spread_one, normed_one)
    back_one = back_one.astype(jnp.bfloat16)
    grad_conv_one = jnp.concatenate([jnp.dot(first_tap.T, back_one, preferred_element_type=jnp.float32), jnp.dot(second_tap.T, back_one, preferred_element_type=jnp.float32), jnp.dot(third_tap.T, back_one, preferred_element_type=jnp.float32)], axis=0)
    to_first = jnp.dot(back_one, conv_one[:width].T, preferred_element_type=jnp.float32)
    to_second = jnp.dot(back_one, conv_one[width:2 * width].T, preferred_element_type=jnp.float32)
    to_third = jnp.dot(back_one, conv_one[2 * width:].T, preferred_element_type=jnp.float32)
    even_grad = to_first + jnp.concatenate([jnp.zeros((1, width), jnp.float32), to_third[:-1]], axis=0)
    frame_grad = jnp.stack([even_grad, to_second], axis=1).reshape(2 * frames_one, width)
    return (act_one.astype(jnp.bfloat16), grad_conv_one, grad_gain_one, grad_bias_one, frame_grad, to_third[-1:])

def assemble(audio_blocks, send_list, place_list):
    source = place_list // CAP
    slot_ids = place_list % CAP
    store_ids = jnp.arange(N_SEQ, dtype=jnp.int32)[:, None, None]
    dest_ids = jnp.arange(N_DP, dtype=jnp.int32)[None, :, None]
    local_ids = send_list[store_ids, source, dest_ids * CAP + slot_ids]
    gathered = audio_blocks[source, store_ids * ROWS + local_ids]
    return jnp.transpose(gathered, (1, 0, 2, 3)).reshape(N_DP, N_SEQ * ROWS * BLEN)

def reference(audio_blocks, send_list, place_list, cotangent, conv_zero, conv_one, gain_zero, bias_zero, gain_one, bias_one):
    waveforms = assemble(audio_blocks, send_list, place_list)

    def utterance(totals, inputs):
        waveform, upstream = inputs
        frames_zero = waveform.shape[0] // 5
        padded = jnp.concatenate([waveform, jnp.zeros((5,), jnp.bfloat16)])
        patches = frame_patches(padded, frames_zero)
        pre_zero = jnp.dot(patches, conv_zero, preferred_element_type=jnp.float32)
        act_zero, scaled_zero, spread_zero, normed_zero = norm_forward(pre_zero, gain_zero, bias_zero)
        frames_in = jnp.concatenate([act_zero.astype(jnp.bfloat16), jnp.zeros((1, C), jnp.bfloat16)], axis=0)
        feats, grad_one, gain_one_grad, bias_one_grad, frame_grad, tail_grad = layer_one(frames_in, frames_zero // 2, conv_one, gain_one, bias_one, upstream)
        back_zero, gain_zero_grad, bias_zero_grad = norm_backward(frame_grad, gain_zero, scaled_zero, spread_zero, normed_zero)
        grad_zero = jnp.dot(patches.astype(jnp.float32).T, back_zero, precision=lax.Precision.HIGHEST)
        totals = (totals[0] + grad_one, totals[1] + grad_zero, totals[2] + gain_zero_grad, totals[3] + bias_zero_grad, totals[4] + gain_one_grad, totals[5] + bias_one_grad)
        return (totals, feats)
    start = (jnp.zeros((3 * C, C), jnp.float32), jnp.zeros((10, C), jnp.float32), jnp.zeros((C,), jnp.float32), jnp.zeros((C,), jnp.float32), jnp.zeros((C,), jnp.float32), jnp.zeros((C,), jnp.float32))
    totals, features = lax.scan(utterance, start, (waveforms, cotangent))
    return (features, totals[0], totals[1], totals[2], totals[3], totals[4], totals[5])
```

```python
import functools

import jax
import jax.numpy as jnp
from jax import lax
from jax.experimental import pallas as pl
from jax.experimental.pallas import tpu as pltpu
from jax.sharding import PartitionSpec as P

MESH = pl.DeviceIdType.MESH
F32 = jnp.float32
BF16 = jnp.bfloat16
norm_eps = 1e-05
n_core = 2
n_y = 8
slots = 4
group = 64
lanes = slots * group
chunk_rows = 64
tail_rows = 16


def iota(shape, dim):
    return lax.broadcasted_iota(jnp.int32, shape, dim)


def one_hot(mask):
    return jnp.where(mask, 1.0, 0.0).astype(BF16)


def dot(a, b, dims=((1,), (0,))):
    return lax.dot_general(a, b, (dims, ((), ())), preferred_element_type=F32)


TN = ((0,), (0,))
NT = ((1,), (1,))


def norm_gelu(pre, gain, bias):
    center = pre - jnp.mean(pre, axis=-1, keepdims=True)
    spread = lax.rsqrt(jnp.mean(center * center, axis=-1, keepdims=True) + norm_eps)
    scaled = center * spread
    normed = scaled * gain + bias
    below = 0.5 + 0.5 * lax.erf(normed * 0.7071067811865476)
    act = normed * below
    slope = below + normed * (jnp.exp(-0.5 * normed * normed) * 0.3989422804014327)
    return act, scaled, spread, slope


def norm_back(upstream, gain, scaled, spread, slope):
    inner = upstream * slope
    pushed = inner * gain
    back = spread * (
        pushed
        - jnp.mean(pushed, axis=-1, keepdims=True)
        - scaled * jnp.mean(pushed * scaled, axis=-1, keepdims=True)
    )
    return back, inner * scaled, inner


def fold_rows(array):
    return jnp.sum(array.reshape(array.shape[0] // 8, 8, array.shape[1]), axis=0)


def kernel(
    sizes,
    audio_ref,
    send_ref,
    place_ref,
    cot_ref,
    wz_ref,
    w_ref,
    gz_ref,
    bz_ref,
    g1_ref,
    b1_ref,
    feats_ref,
    grad_ref,
    gwz_ref,
    ggz_ref,
    gbz_ref,
    gg1_ref,
    gb1_ref,
    msg,
    arr,
    own_row,
    rim,
    samples,
    patches,
    wz_pad,
    act_even,
    act_odd,
    scaled_even,
    scaled_odd,
    slope_even,
    slope_odd,
    spread_even,
    spread_odd,
    third,
    back_one,
    back_f32,
    back_down,
    hi_even,
    lo_even,
    hi_odd,
    lo_odd,
    parts,
    got_core,
    sum_core,
    got_x,
    sum_x,
    got_y,
    sum_y,
    got_z,
    small,
    small_core,
    small_x,
    small_y,
    small_z,
    small_half,
    small_full,
    msg_send,
    msg_recv,
    rim_sems,
    core_sems,
    x_send,
    x_recv,
    y_send,
    y_recv,
    z_send,
    z_recv,
    sc_sems,
    sx_send,
    sx_recv,
    sy_send,
    sy_recv,
    sz_send,
    sz_recv,
    sf_sems,
):
    n_dp, n_x, n_z, n_rows, n_out, width = sizes
    n_even = n_out + tail_rows
    me = lax.axis_index("dp")
    z = lax.axis_index("seq")
    core = lax.rem(me, n_core)
    y = lax.rem(me // n_core, n_y)
    x = me // (n_core * n_y)

    def dp_of(px, py, pc):
        return (px * n_y + py) * n_core + pc

    barrier = pltpu.get_barrier_semaphore()

    def greet_dp(k, carry):
        pl.semaphore_signal(
            barrier, inc=1, device_id={"dp": lax.rem(me + k, n_dp)}, device_id_type=MESH
        )
        return carry

    def greet_z(k, carry):
        pl.semaphore_signal(
            barrier, inc=1, device_id={"seq": lax.rem(z + k, n_z)}, device_id_type=MESH
        )
        return carry

    lax.fori_loop(1, n_dp, greet_dp, 0)
    lax.fori_loop(1, n_z, greet_z, 0)

    spread_lanes = one_hot(
        jnp.bitwise_and(iota((40, lanes), 1), group - 1) == iota((40, lanes), 0)
    )
    blocks = dot(audio_ref[...], spread_lanes, TN).astype(BF16)
    chosen = one_hot(iota((n_rows, n_dp * slots), 0) == send_ref[...])
    picked = dot(chosen, blocks, TN)
    slot_of = jnp.bitwise_and(iota((n_dp * slots, lanes), 0), slots - 1)
    lane_group = lax.shift_right_logical(iota((n_dp * slots, lanes), 1), 6)
    in_group = slot_of == lane_group
    picked = jnp.where(in_group, picked, 0.0).astype(BF16)
    gather_dest = one_hot(
        lax.shift_right_logical(iota((n_dp, n_dp * slots), 1), 2) == iota((n_dp, n_dp * slots), 0)
    )
    message = dot(gather_dest, picked)
    for d in range(n_dp):
        msg[d] = message[d : d + 1]

    pl.semaphore_wait(barrier, n_dp - 1 + n_z - 1)

    def msg_copy(k):
        peer = lax.rem(me + k, n_dp)
        return pltpu.make_async_remote_copy(
            src_ref=msg.at[peer],
            dst_ref=arr.at[me],
            send_sem=msg_send.at[k],
            recv_sem=msg_recv.at[k],
            device_id={"dp": peer},
            device_id_type=MESH,
        )

    def start_msg(k, carry):
        msg_copy(k).start()
        return carry

    lax.fori_loop(1, n_dp, start_msg, 0)
    arr[me] = msg[me]

    wz_pad[...] = jnp.zeros_like(wz_pad)
    wz_pad[0:10, :] = wz_ref[...]
    gain_zero, bias_zero = gz_ref[...], bz_ref[...]
    gain_one, bias_one = g1_ref[...], b1_ref[...]
    keep = jnp.where(z < n_z - 1, 1.0, 0.0).astype(F32)
    placed = one_hot(iota((n_dp * slots, n_rows), 0) == place_ref[...])
    spread_slots = one_hot(
        lax.shift_right_logical(iota((n_dp * slots, n_dp), 0), 2) == iota((n_dp * slots, n_dp), 1)
    )
    lane_in, lane_out = iota((lanes, lanes), 0), iota((lanes, lanes), 1)
    sample_in = jnp.bitwise_and(lane_in, group - 1)
    sample_out = jnp.bitwise_and(lane_out, group - 1)
    fold_here = one_hot((sample_in == sample_out) & (sample_out < 40))
    fold_next = one_hot((sample_in + 40 == sample_out) & (sample_out < 45))
    row_id = iota((n_even, n_rows + 8), 0)
    widen = one_hot(lax.shift_right_logical(row_id, 2) == iota((n_even, n_rows + 8), 1))
    phase = jnp.bitwise_and(iota((n_even, lanes), 0), 3)
    own_phase = phase == lax.shift_right_logical(iota((n_even, lanes), 1), 6)
    tap = sample_in - 10 * lax.shift_right_logical(lane_in, 6)
    wanted = jnp.where(lane_out < 128, lane_out, lane_out - 128 + 5)
    limit = jnp.where(lane_out < 128, 10, 15)
    to_patch = one_hot((tap == wanted) & (wanted < limit))

    def wait_msg(k, carry):
        msg_copy(k).wait_recv()
        return carry

    lax.fori_loop(1, n_dp, wait_msg, 0)

    received = jnp.concatenate([arr[s] for s in range(n_dp)], axis=0).astype(BF16)
    by_slot = dot(spread_slots, received)
    by_slot = jnp.where(in_group, by_slot, 0.0).astype(BF16)
    ordered = dot(placed, by_slot, TN)
    own_row[...] = ordered[0:8]
    rim_copy = pltpu.make_async_remote_copy(
        src_ref=own_row,
        dst_ref=rim,
        send_sem=rim_sems.at[0],
        recv_sem=rim_sems.at[1],
        device_id={"seq": lax.rem(z + n_z - 1, n_z)},
        device_id_type=MESH,
    )
    rim_copy.start()
    samples[0:n_rows, :] = ordered
    samples[n_rows : n_rows + 16, :] = jnp.zeros((16, lanes), F32)
    rim_copy.wait_recv()
    rim_lane = jnp.bitwise_and(iota((8, lanes), 1), group - 1)
    rim_row = iota((8, lanes), 0)
    samples[n_rows : n_rows + 8, :] = jnp.where(
        (rim_row == 0) & (rim_lane < 10), rim[...] * keep, 0.0
    )

    wide = dot(samples[0 : n_rows + 8, :].astype(BF16), fold_here) + dot(
        samples[1 : n_rows + 9, :].astype(BF16), fold_next
    )
    rows = dot(widen, wide.astype(BF16))
    rows = jnp.where(own_phase, rows, 0.0).astype(BF16)
    patches[...] = dot(rows, to_patch).astype(BF16)

    def forward_even(r, n):
        pre = dot(patches[pl.ds(r, n), 0:128], wz_pad[...])
        act, scaled, spread, slope = norm_gelu(pre, gain_zero, bias_zero)
        scaled_even[pl.ds(r, n), :] = scaled
        slope_even[pl.ds(r, n), :] = slope
        spread_even[pl.ds(r, n), :] = spread
        return act

    def forward_zero(i, carry):
        r = pl.multiple_of(i * chunk_rows, chunk_rows)
        act_even[pl.ds(r, chunk_rows), :] = forward_even(r, chunk_rows).astype(BF16)
        pre = dot(patches[pl.ds(r, chunk_rows), 128:256], wz_pad[...])
        act, scaled, spread, slope = norm_gelu(pre, gain_zero, bias_zero)
        act_odd[pl.ds(r, chunk_rows), :] = act.astype(BF16)
        scaled_odd[pl.ds(r, chunk_rows), :] = scaled
        slope_odd[pl.ds(r, chunk_rows), :] = slope
        spread_odd[pl.ds(r, chunk_rows), :] = spread
        return carry

    lax.fori_loop(0, n_out // chunk_rows, forward_zero, 0)
    act_even[n_out:n_even, :] = (forward_even(n_out, tail_rows) * keep).astype(BF16)

    third[...] = dot(act_even[...], w_ref[2 * width : 3 * width, :])
    third[0:n_out, :] = third[1 : n_out + 1, :]

    def layer_one(i, carry):
        sum_gain, sum_bias = carry
        r = pl.multiple_of(i * chunk_rows, chunk_rows)
        here = pl.ds(r, chunk_rows)
        pre = (
            dot(act_even[here, :], w_ref[0:width, :])
            + dot(act_odd[here, :], w_ref[width : 2 * width, :])
            + third[here, :]
        )
        act, scaled, spread, slope = norm_gelu(pre, gain_one, bias_one)
        feats_ref[here, :] = act.astype(BF16)
        back, gain_term, bias_term = norm_back(
            cot_ref[here, :].astype(F32), gain_one, scaled, spread, slope
        )
        back = back.astype(BF16)
        back_one[here, :] = back
        back_f32[pl.ds(r + 8, chunk_rows), :] = back.astype(F32)
        return (sum_gain + fold_rows(gain_term), sum_bias + fold_rows(bias_term))

    zero_sum = jnp.zeros((8, width), F32)
    back_f32[0:8, :] = jnp.zeros((8, width), F32)
    back_f32[n_out + 8 :, :] = jnp.zeros((back_f32.shape[0] - n_out - 8, width), F32)
    sum_gain_one, sum_bias_one = lax.fori_loop(
        0, n_out // chunk_rows, layer_one, (zero_sum, zero_sum)
    )
    back_down[...] = back_f32[7 : 7 + n_even, :].astype(BF16)

    per_owner = 3 * width // 8 // n_dp

    def keep_pages(first_page, value):
        for i in range(width // 8):
            page = first_page + i
            d, j = page // per_owner, page % per_owner
            px, py, pc = d // (n_core * n_y), (d // n_core) % n_y, d % n_core
            at = ((pc * n_x + px) * n_y + py) * per_owner + j
            parts[at] = value[8 * i : 8 * i + 8, :].astype(BF16)

    keep_pages(0, dot(act_even[0:n_out, :], back_one[...], TN))
    keep_pages(width // 8, dot(act_odd[...], back_one[...], TN))
    keep_pages(2 * width // 8, dot(act_even[...], back_down[...], TN))

    half = n_x * n_y * per_owner
    x_part = n_y * per_owner
    core_copy = pltpu.make_async_remote_copy(
        src_ref=parts.at[pl.ds((1 - core) * half, half)],
        dst_ref=got_core,
        send_sem=core_sems.at[0],
        recv_sem=core_sems.at[1],
        device_id={"dp": dp_of(x, y, 1 - core)},
        device_id_type=MESH,
    )
    core_copy.start()

    def back_zero(r, n, upstream, scaled_ref, slope_ref, spread_ref, hi_ref, lo_ref):
        here = pl.ds(r, n)
        back, gain_term, bias_term = norm_back(
            upstream, gain_zero, scaled_ref[here, :], spread_ref[here, :], slope_ref[here, :]
        )
        hi = back.astype(BF16)
        hi_ref[here, :] = hi
        lo_ref[here, :] = (back - hi.astype(F32)).astype(BF16)
        return fold_rows(gain_term), fold_rows(bias_term)

    def back_even(i, carry):
        r = pl.multiple_of(i * chunk_rows, chunk_rows)
        here = pl.ds(r, chunk_rows)
        upstream = dot(back_one[here, :], w_ref[0:width, :], NT) + dot(
            back_down[here, :], w_ref[2 * width : 3 * width, :], NT
        )
        terms = back_zero(
            r, chunk_rows, upstream, scaled_even, slope_even, spread_even, hi_even, lo_even
        )
        return (carry[0] + terms[0], carry[1] + terms[1])

    def back_odd(i, carry):
        r = pl.multiple_of(i * chunk_rows, chunk_rows)
        here = pl.ds(r, chunk_rows)
        upstream = dot(back_one[here, :], w_ref[width : 2 * width, :], NT)
        terms = back_zero(
            r, chunk_rows, upstream, scaled_odd, slope_odd, spread_odd, hi_odd, lo_odd
        )
        return (carry[0] + terms[0], carry[1] + terms[1])

    sums = lax.fori_loop(0, n_out // chunk_rows, back_even, (zero_sum, zero_sum))
    upstream = (
        dot(back_down[n_out:n_even, :], w_ref[2 * width : 3 * width, :], NT) * keep
    )
    terms = back_zero(
        n_out, tail_rows, upstream, scaled_even, slope_even, spread_even, hi_even, lo_even
    )
    sums = (sums[0] + terms[0], sums[1] + terms[1])

    core_copy.wait_recv()
    mine = core * half

    def add_core(i, carry):
        at = pl.multiple_of(i * per_owner, per_owner)
        total = parts[pl.ds(mine + at, per_owner)].astype(F32) + got_core[
            pl.ds(at, per_owner)
        ].astype(F32)
        sum_core[pl.ds(at, per_owner)] = total.astype(BF16)
        return carry

    lax.fori_loop(0, half // per_owner, add_core, 0)

    def x_copy(k):
        peer = lax.rem(x + k, n_x)
        return pltpu.make_async_remote_copy(
            src_ref=sum_core.at[pl.ds(peer * x_part, x_part)],
            dst_ref=got_x.at[k],
            send_sem=x_send.at[k],
            recv_sem=x_recv.at[k],
            device_id={"dp": dp_of(peer, y, core)},
            device_id_type=MESH,
        )

    for k in range(1, n_x):
        x_copy(k).start()

    sums = lax.fori_loop(0, n_out // chunk_rows, back_odd, sums)

    grad_wz = (
        dot(patches[:, 0:128], hi_even[...], TN)
        + dot(patches[:, 0:128], lo_even[...], TN)
        + dot(patches[0:n_out, 128:256], hi_odd[...], TN)
        + dot(patches[0:n_out, 128:256], lo_odd[...], TN)
    )

    def row_sum(array):
        return jnp.sum(array, axis=0, keepdims=True)

    small[0, :, :] = grad_wz[0:8]
    small[1, 0:2, :] = grad_wz[8:10]
    small[1, 2:3, :] = row_sum(sums[0])
    small[1, 3:4, :] = row_sum(sums[1])
    small[1, 4:5, :] = row_sum(sum_gain_one)
    small[1, 5:6, :] = row_sum(sum_bias_one)
    small[1, 6:8, :] = jnp.zeros((2, width), F32)
    small_core_copy = pltpu.make_async_remote_copy(
        src_ref=small.at[1 - core],
        dst_ref=small_core,
        send_sem=sc_sems.at[0],
        recv_sem=sc_sems.at[1],
        device_id={"dp": dp_of(x, y, 1 - core)},
        device_id_type=MESH,
    )
    small_core_copy.start()
    small_core_copy.wait_recv()
    small_x[x] = small[core] + small_core[...]

    def sx_copy(k):
        return pltpu.make_async_remote_copy(
            src_ref=small_x.at[x],
            dst_ref=small_x.at[x],
            send_sem=sx_send.at[k],
            recv_sem=sx_recv.at[k],
            device_id={"dp": dp_of(lax.rem(x + k, n_x), y, core)},
            device_id_type=MESH,
        )

    for k in range(1, n_x):
        sx_copy(k).start()

    for k in range(1, n_x):
        x_copy(k).wait_recv()

    def add_x(i, carry):
        at = pl.multiple_of(i * per_owner, per_owner)
        here = pl.ds(at, per_owner)
        total = sum_core[pl.ds(x * x_part + at, per_owner)].astype(F32)
        for k in range(1, n_x):
            total = total + got_x[k, here].astype(F32)
        sum_x[here] = total.astype(BF16)
        return carry

    lax.fori_loop(0, n_y, add_x, 0)

    def y_copy(k):
        peer = lax.rem(y + k, n_y)
        return pltpu.make_async_remote_copy(
            src_ref=sum_x.at[pl.ds(peer * per_owner, per_owner)],
            dst_ref=got_y.at[k],
            send_sem=y_send.at[k],
            recv_sem=y_recv.at[k],
            device_id={"dp": dp_of(x, peer, core)},
            device_id_type=MESH,
        )

    for k in range(1, n_y):
        y_copy(k).start()

    for k in range(1, n_x):
        sx_copy(k).wait_recv()
    total = small_x[0]
    for k in range(1, n_x):
        total = total + small_x[k]
    small_y[y] = total

    def sy_copy(k):
        return pltpu.make_async_remote_copy(
            src_ref=small_y.at[y],
            dst_ref=small_y.at[y],
            send_sem=sy_send.at[k],
            recv_sem=sy_recv.at[k],
            device_id={"dp": dp_of(x, lax.rem(y + k, n_y), core)},
            device_id_type=MESH,
        )

    for k in range(1, n_y):
        sy_copy(k).start()

    for k in range(1, n_y):
        y_copy(k).wait_recv()
    total = sum_x[pl.ds(y * per_owner, per_owner)].astype(F32)
    for k in range(1, n_y):
        total = total + got_y[k].astype(F32)
    got_z[z] = total.astype(BF16)

    def z_copy(k):
        return pltpu.make_async_remote_copy(
            src_ref=got_z.at[z],
            dst_ref=got_z.at[z],
            send_sem=z_send.at[k],
            recv_sem=z_recv.at[k],
            device_id={"seq": lax.rem(z + k, n_z)},
            device_id_type=MESH,
        )

    order_z = sorted(range(1, n_z), key=lambda k: -min(k, n_z - k))
    for k in order_z:
        z_copy(k).start()

    for k in range(1, n_y):
        sy_copy(k).wait_recv()
    total = small_y[0]
    for k in range(1, n_y):
        total = total + small_y[k]
    small_z[z] = total.astype(BF16)

    def sz_copy(k):
        return pltpu.make_async_remote_copy(
            src_ref=small_z.at[z],
            dst_ref=small_z.at[z],
            send_sem=sz_send.at[k],
            recv_sem=sz_recv.at[k],
            device_id={"seq": lax.rem(z + k, n_z)},
            device_id_type=MESH,
        )

    for k in order_z:
        sz_copy(k).start()

    for k in range(1, n_z):
        z_copy(k).wait_recv()
    total = got_z[0].astype(F32)
    for k in range(1, n_z):
        total = total + got_z[k].astype(F32)
    for j in range(per_owner):
        grad_ref[8 * j : 8 * j + 8, :] = total[j]

    for k in range(1, n_z):
        sz_copy(k).wait_recv()
    total = small_z[0].astype(F32)
    for k in range(1, n_z):
        total = total + small_z[k].astype(F32)
    small_half[...] = total
    full_copy = pltpu.make_async_remote_copy(
        src_ref=small_half,
        dst_ref=small_full.at[core],
        send_sem=sf_sems.at[0],
        recv_sem=sf_sems.at[1],
        device_id={"dp": dp_of(x, y, 1 - core)},
        device_id_type=MESH,
    )
    full_copy.start()
    small_full[core] = total
    full_copy.wait_recv()
    gwz_ref[0:8, :] = small_full[0]
    rest = small_full[1]
    gwz_ref[8:10, :] = rest[0:2]
    ggz_ref[...] = rest[2:3]
    gbz_ref[...] = rest[3:4]
    gg1_ref[...] = rest[4:5]
    gb1_ref[...] = rest[5:6]

    def sent_msg(k, carry):
        msg_copy(k).wait_send()
        return carry

    lax.fori_loop(1, n_dp, sent_msg, 0)
    rim_copy.wait_send()
    core_copy.wait_send()
    small_core_copy.wait_send()
    full_copy.wait_send()
    for k in range(1, n_x):
        x_copy(k).wait_send()
        sx_copy(k).wait_send()
    for k in range(1, n_y):
        y_copy(k).wait_send()
        sy_copy(k).wait_send()
    for k in range(1, n_z):
        z_copy(k).wait_send()
        sz_copy(k).wait_send()


def on_device(n_dp, n_z, audio, send, place, cot, conv_zero, conv_one, gz, bz, g1, b1):
    n_x = n_dp // (n_core * n_y)
    n_rows, n_out, width = audio.shape[1], cot.shape[1], cot.shape[2]
    n_even = n_out + tail_rows
    per_owner = 3 * width // 8 // n_dp
    pages = 3 * width // 8
    vmem = lambda *shape, dtype=F32: pltpu.VMEM(shape, dtype)
    dma = lambda n: pltpu.SemaphoreType.DMA((n,))
    scratch = [
        vmem(n_dp, 1, lanes),
        vmem(n_dp, 1, lanes),
        vmem(8, lanes),
        vmem(8, lanes),
        vmem(n_rows + 16, lanes),
        vmem(n_even, lanes, dtype=BF16),
        vmem(128, width, dtype=BF16),
        vmem(n_even, width, dtype=BF16),
        vmem(n_out, width, dtype=BF16),
        vmem(n_even, width),
        vmem(n_out, width),
        vmem(n_even, width),
        vmem(n_out, width),
        vmem(n_even, 1),
        vmem(n_out, 1),
        vmem(n_even, width),
        vmem(n_out, width, dtype=BF16),
        vmem(n_out + 32, width),
        vmem(n_even, width, dtype=BF16),
        vmem(n_even, width, dtype=BF16),
        vmem(n_even, width, dtype=BF16),
        vmem(n_out, width, dtype=BF16),
        vmem(n_out, width, dtype=BF16),
        vmem(pages, 8, width, dtype=BF16),
        vmem(pages // 2, 8, width, dtype=BF16),
        vmem(pages // 2, 8, width, dtype=BF16),
        vmem(n_x, n_y * per_owner, 8, width, dtype=BF16),
        vmem(n_y * per_owner, 8, width, dtype=BF16),
        vmem(n_y, per_owner, 8, width, dtype=BF16),
        vmem(8, width),
        vmem(n_z, per_owner, 8, width, dtype=BF16),
        vmem(2, 8, width),
        vmem(8, width),
        vmem(n_x, 8, width),
        vmem(n_y, 8, width),
        vmem(n_z, 8, width, dtype=BF16),
        vmem(8, width),
        vmem(2, 8, width),
        dma(n_dp),
        dma(n_dp),
        dma(2),
        dma(2),
        dma(n_x),
        dma(n_x),
        dma(n_y),
        dma(n_y),
        dma(n_z),
        dma(n_z),
        dma(2),
        dma(n_x),
        dma(n_x),
        dma(n_y),
        dma(n_y),
        dma(n_z),
        dma(n_z),
        dma(2),
    ]
    row = jax.ShapeDtypeStruct((1, width), F32)
    outs = pl.pallas_call(
        functools.partial(kernel, (n_dp, n_x, n_z, n_rows, n_out, width)),
        out_shape=(
            jax.ShapeDtypeStruct((n_out, width), BF16),
            jax.ShapeDtypeStruct((3 * width // n_dp, width), F32),
            jax.ShapeDtypeStruct((10, width), F32),
            row,
            row,
            row,
            row,
        ),
        in_specs=[pl.BlockSpec(memory_space=pltpu.VMEM)] * 10,
        out_specs=(pl.BlockSpec(memory_space=pltpu.VMEM),) * 7,
        scratch_shapes=scratch,
        compiler_params=pltpu.CompilerParams(
            collective_id=0, has_side_effects=True, vmem_limit_bytes=56 * 2**20
        ),
    )(
        audio[0].T,
        send.reshape(1, -1),
        place.reshape(1, -1),
        cot[0],
        conv_zero,
        conv_one,
        gz[None],
        bz[None],
        g1[None],
        b1[None],
    )
    feats, grad, gwz, ggz, gbz, gg1, gb1 = outs
    return feats[None], grad, gwz, ggz[0], gbz[0], gg1[0], gb1[0]


def solution(mesh):
    placed = (
        P("dp", "seq", None),
        P("seq", "dp", None),
        P("seq", "dp", None),
        P("dp", "seq", None),
        P(),
        P(),
        P(),
        P(),
        P(),
        P(),
    )
    return jax.shard_map(
        functools.partial(on_device, mesh.shape["dp"], mesh.shape["seq"]),
        mesh=mesh,
        in_specs=placed,
        out_specs=(P("dp", "seq", None), P("dp", None), P(), P(), P(), P(), P()),
        check_vma=False,
    )
```

```python
import functools

import jax
import jax.numpy as jnp
from jax import lax
from jax.experimental import pallas as pl
from jax.experimental.pallas import tpu as pltpu
from jax.sharding import PartitionSpec as P

MESH = pl.DeviceIdType.MESH
F32 = jnp.float32
BF16 = jnp.bfloat16
norm_eps = 1e-05
n_core = 2
n_y = 8
slots = 4
group = 64
lanes = slots * group
chunk_zero = 64
chunk_one = 128
chunk_back = 128
tail_rows = 16


def iota(shape, dim):
    return lax.broadcasted_iota(jnp.int32, shape, dim)


def one_hot(mask):
    return jnp.where(mask, 1.0, 0.0).astype(BF16)


def dot(a, b, dims=((1,), (0,))):
    return lax.dot_general(a, b, (dims, ((), ())), preferred_element_type=F32)


TN = ((0,), (0,))
NT = ((1,), (1,))


def norm_gelu(pre, gain, bias):
    center = pre - jnp.mean(pre, axis=-1, keepdims=True)
    spread = lax.rsqrt(jnp.mean(center * center, axis=-1, keepdims=True) + norm_eps)
    scaled = center * spread
    normed = scaled * gain + bias
    below = 0.5 + 0.5 * lax.erf(normed * 0.7071067811865476)
    act = normed * below
    slope = below + normed * (jnp.exp(-0.5 * normed * normed) * 0.3989422804014327)
    return act, scaled, spread, slope


def norm_back(upstream, gain, scaled, spread, slope):
    inner = upstream * slope
    pushed = inner * gain
    back = spread * (
        pushed
        - jnp.mean(pushed, axis=-1, keepdims=True)
        - scaled * jnp.mean(pushed * scaled, axis=-1, keepdims=True)
    )
    return back, inner * scaled, inner


def fold_rows(array):
    return jnp.sum(array.reshape(array.shape[0] // 8, 8, array.shape[1]), axis=0)


def kernel(
    sizes,
    audio_ref,
    send_ref,
    place_ref,
    cot_hbm,
    wz_ref,
    w_hbm,
    gz_ref,
    bz_ref,
    g1_ref,
    b1_ref,
    feats_hbm,
    grad_ref,
    small_full,
    cot_ref,
    w_ref,
    feats_ref,
    msg,
    got_msg,
    arr,
    own_row,
    rim,
    samples,
    patches,
    wz_pad,
    act_even,
    act_odd,
    scaled_even,
    scaled_odd,
    slope_even,
    slope_odd,
    spread_even,
    spread_odd,
    third,
    back_one,
    back_f32,
    back_down,
    hi_even,
    lo_even,
    hi_odd,
    lo_odd,
    parts,
    got_core,
    sum_core,
    got_x,
    sum_x,
    got_y,
    got_z,
    small,
    small_core,
    small_x,
    small_y,
    small_z,
    small_half,
    load_sems,
    near_send,
    near_recv,
    far_send,
    far_recv,
    rim_sems,
    core_send,
    core_recv,
    x_send,
    x_recv,
    y_send,
    y_recv,
    z_send,
    z_recv,
    sc_sems,
    sx_send,
    sx_recv,
    sy_send,
    sy_recv,
    sz_send,
    sz_recv,
    sf_sems,
):
    n_dp, n_x, n_z, n_rows, n_out, width = sizes
    n_even = n_out + tail_rows
    me = lax.axis_index("dp")
    z = lax.axis_index("seq")
    core = lax.rem(me, n_core)
    y = lax.rem(me // n_core, n_y)
    x = me // (n_core * n_y)

    def dp_of(px, py, pc):
        return (px * n_y + py) * n_core + pc

    n_near = n_x * n_core
    near = x * n_core + core

    def near_peer(k):
        at = lax.rem(near + k, n_near)
        return at, dp_of(at // n_core, y, lax.rem(at, n_core))

    def y_peer(k):
        at = lax.rem(y + k, n_y)
        return at, dp_of(x, at, core)

    barrier = pltpu.get_barrier_semaphore()

    def greet(axis, device):
        pl.semaphore_signal(barrier, inc=1, device_id={axis: device}, device_id_type=MESH)

    for k in range(1, n_near):
        greet("dp", near_peer(k)[1])
    for k in range(1, n_y):
        greet("dp", y_peer(k)[1])
    for k in range(1, n_z):
        greet("seq", lax.rem(z + k, n_z))

    load_w = pltpu.make_async_copy(w_hbm, w_ref, load_sems.at[0])
    load_cot = pltpu.make_async_copy(cot_hbm, cot_ref, load_sems.at[1])
    load_w.start()
    load_cot.start()

    spread_lanes = one_hot(
        jnp.bitwise_and(iota((40, lanes), 1), group - 1) == iota((40, lanes), 0)
    )
    blocks = dot(audio_ref[...], spread_lanes, TN).astype(BF16)
    chosen = one_hot(iota((n_rows, n_dp * slots), 0) == send_ref[...])
    picked = dot(chosen, blocks, TN)
    slot_of = jnp.bitwise_and(iota((n_dp * slots, lanes), 0), slots - 1)
    lane_group = lax.shift_right_logical(iota((n_dp * slots, lanes), 1), 6)
    in_group = slot_of == lane_group
    picked = jnp.where(in_group, picked, 0.0).astype(BF16)
    bit_y = n_y.bit_length() - 1

    def of_slot(shape, dim):
        device = lax.shift_right_logical(iota(shape, dim), 2)
        at_core = jnp.bitwise_and(device, n_core - 1)
        at_y = jnp.bitwise_and(lax.shift_right_logical(device, 1), n_y - 1)
        return lax.shift_right_logical(device, 1 + bit_y) * n_core + at_core, at_y

    slot_near, slot_y = of_slot((n_dp, n_dp * slots), 1)
    gather_dest = one_hot(slot_near * n_y + slot_y == iota((n_dp, n_dp * slots), 0))
    message = dot(gather_dest, picked)
    for d in range(n_dp):
        msg[d // n_y, d % n_y] = message[d : d + 1]

    pl.semaphore_wait(barrier, n_near - 1 + n_y - 1 + n_z - 1)

    def near_copy(k):
        at, device = near_peer(k)
        return pltpu.make_async_remote_copy(
            src_ref=msg.at[at],
            dst_ref=got_msg.at[near],
            send_sem=near_send.at[k],
            recv_sem=near_recv.at[k],
            device_id={"dp": device},
            device_id_type=MESH,
        )

    for k in range(1, n_near):
        near_copy(k).start()
    got_msg[near] = msg[near]

    wz_pad[...] = jnp.zeros_like(wz_pad)
    wz_pad[0:10, :] = wz_ref[...]
    gain_zero, bias_zero = gz_ref[...], bz_ref[...]
    gain_one, bias_one = g1_ref[...], b1_ref[...]
    keep = jnp.where(z < n_z - 1, 1.0, 0.0).astype(F32)
    placed = one_hot(iota((n_dp * slots, n_rows), 0) == place_ref[...])
    slot_near, slot_y = of_slot((n_dp * slots, n_dp), 0)
    spread_slots = one_hot(slot_y * n_near + slot_near == iota((n_dp * slots, n_dp), 1))
    lane_in, lane_out = iota((lanes, lanes), 0), iota((lanes, lanes), 1)
    sample_in = jnp.bitwise_and(lane_in, group - 1)
    sample_out = jnp.bitwise_and(lane_out, group - 1)
    fold_here = one_hot((sample_in == sample_out) & (sample_out < 40))
    fold_next = one_hot((sample_in + 40 == sample_out) & (sample_out < 45))
    row_id = iota((n_out, n_rows), 0)
    widen = one_hot(lax.shift_right_logical(row_id, 2) == iota((n_out, n_rows), 1))
    phase = jnp.bitwise_and(iota((n_out, lanes), 0), 3)
    own_phase = phase == lax.shift_right_logical(iota((n_out, lanes), 1), 6)
    tap = sample_in - 10 * lax.shift_right_logical(lane_in, 6)
    wanted = jnp.where(lane_out < 128, lane_out, lane_out - 128 + 5)
    limit = jnp.where(lane_out < 128, 10, 15)
    to_patch = one_hot((tap == wanted) & (wanted < limit))
    edge_from = jnp.where(lane_out < 128, lane_out, lane_out - 133)
    edge_limit = jnp.where(lane_out < 128, 10, 5)
    to_edge = one_hot((sample_in == edge_from) & (edge_from < edge_limit))

    for k in range(1, n_near):
        near_copy(k).wait_recv()

    def far_copy(k):
        at, device = y_peer(k)
        return pltpu.make_async_remote_copy(
            src_ref=got_msg.at[:, at],
            dst_ref=arr.at[y],
            send_sem=far_send.at[k],
            recv_sem=far_recv.at[k],
            device_id={"dp": device},
            device_id_type=MESH,
        )

    order_y = sorted(range(1, n_y), key=lambda k: -min(k, n_y - k))
    order_z = sorted(range(1, n_z), key=lambda k: -min(k, n_z - k))
    for k in order_y:
        far_copy(k).start()
    arr[y] = got_msg[:, y]
    for k in range(1, n_y):
        far_copy(k).wait_recv()

    received = jnp.concatenate(
        [arr[s // n_near, s % n_near] for s in range(n_dp)], axis=0
    ).astype(BF16)
    by_slot = dot(spread_slots, received)
    by_slot = jnp.where(in_group, by_slot, 0.0).astype(BF16)
    ordered = dot(placed, by_slot, TN)
    own_row[...] = dot(ordered[0:8].astype(BF16), to_edge)
    rim_copy = pltpu.make_async_remote_copy(
        src_ref=own_row,
        dst_ref=rim,
        send_sem=rim_sems.at[0],
        recv_sem=rim_sems.at[1],
        device_id={"seq": lax.rem(z + n_z - 1, n_z)},
        device_id_type=MESH,
    )
    rim_copy.start()
    samples[0:n_rows, :] = ordered
    samples[n_rows : n_rows + 8, :] = jnp.zeros((8, lanes), F32)
    wide = dot(samples[0:n_rows, :].astype(BF16), fold_here) + dot(
        samples[1 : n_rows + 1, :].astype(BF16), fold_next
    )
    rows = dot(widen, wide.astype(BF16))
    rows = jnp.where(own_phase, rows, 0.0).astype(BF16)
    patches[0:n_out, :] = dot(rows, to_patch).astype(BF16)

    def forward_even(r, n):
        pre = dot(patches[pl.ds(r, n), 0:128], wz_pad[...])
        act, scaled, spread, slope = norm_gelu(pre, gain_zero, bias_zero)
        scaled_even[pl.ds(r, n), :] = scaled
        slope_even[pl.ds(r, n), :] = slope
        spread_even[pl.ds(r, n), :] = spread
        return act

    def forward_odd(r, n):
        pre = dot(patches[pl.ds(r, n), 128:256], wz_pad[...])
        act, scaled, spread, slope = norm_gelu(pre, gain_zero, bias_zero)
        act_odd[pl.ds(r, n), :] = act.astype(BF16)
        scaled_odd[pl.ds(r, n), :] = scaled
        slope_odd[pl.ds(r, n), :] = slope
        spread_odd[pl.ds(r, n), :] = spread

    def forward_zero(i, carry):
        r = pl.multiple_of(i * chunk_zero, chunk_zero)
        act_even[pl.ds(r, chunk_zero), :] = forward_even(r, chunk_zero).astype(BF16)
        forward_odd(r, chunk_zero)
        return carry

    lax.fori_loop(0, n_out // chunk_zero, forward_zero, 0)

    rim_copy.wait_recv()
    edge = rim[0:1, :] * keep
    tail_id = iota((tail_rows, 128), 0)
    last = pl.ds(n_out - tail_rows, tail_rows)
    patches[last, 128:256] = (
        patches[last, 128:256].astype(F32)
        + jnp.where(tail_id == tail_rows - 1, edge[:, 128:256], 0.0)
    ).astype(BF16)
    patches[n_out:n_even, 0:128] = jnp.where(tail_id == 0, edge[:, 0:128], 0.0).astype(BF16)
    forward_odd(n_out - tail_rows, tail_rows)
    act_even[n_out:n_even, :] = (forward_even(n_out, tail_rows) * keep).astype(BF16)
    load_w.wait()

    third[...] = dot(act_even[...], w_ref[2 * width : 3 * width, :])
    for r in range(0, n_out, 64):
        third[r : r + 64, :] = third[r + 1 : r + 65, :]
    load_cot.wait()

    def layer_one(i, carry):
        sum_gain, sum_bias = carry
        r = pl.multiple_of(i * chunk_one, chunk_one)
        here = pl.ds(r, chunk_one)
        pre = (
            dot(act_even[here, :], w_ref[0:width, :])
            + dot(act_odd[here, :], w_ref[width : 2 * width, :])
            + third[here, :]
        )
        act, scaled, spread, slope = norm_gelu(pre, gain_one, bias_one)
        feats_ref[here, :] = act.astype(BF16)
        back, gain_term, bias_term = norm_back(
            cot_ref[here, :].astype(F32), gain_one, scaled, spread, slope
        )
        back = back.astype(BF16)
        back_one[here, :] = back
        back_f32[pl.ds(r + 8, chunk_one), :] = back.astype(F32)
        return (sum_gain + fold_rows(gain_term), sum_bias + fold_rows(bias_term))

    zero_sum = jnp.zeros((8, width), F32)
    back_f32[0:8, :] = jnp.zeros((8, width), F32)
    back_f32[n_out + 8 :, :] = jnp.zeros((back_f32.shape[0] - n_out - 8, width), F32)
    sum_gain_one, sum_bias_one = lax.fori_loop(
        0, n_out // chunk_one, layer_one, (zero_sum, zero_sum)
    )
    back_down[...] = back_f32[7 : 7 + n_even, :].astype(BF16)

    keep_feats = pltpu.make_async_copy(feats_ref, feats_hbm, load_sems.at[2])
    keep_feats.start()

    per_owner = 3 * width // 8 // n_dp

    def keep_pages(first_page, value):
        for i in range(width // 8):
            page = first_page + i
            d, j = page // per_owner, page % per_owner
            px, py, pc = d // (n_core * n_y), (d // n_core) % n_y, d % n_core
            parts[j, pc, px * n_y + py] = value[8 * i : 8 * i + 8, :].astype(BF16)

    keep_pages(0, dot(act_even[0:n_out, :], back_one[...], TN))
    keep_pages(width // 8, dot(act_odd[...], back_one[...], TN))
    keep_pages(2 * width // 8, dot(act_even[...], back_down[...], TN))

    partner = dp_of(x, y, 1 - core)

    def core_copy(j):
        return pltpu.make_async_remote_copy(
            src_ref=parts.at[j, 1 - core],
            dst_ref=got_core.at[j],
            send_sem=core_send.at[j],
            recv_sem=core_recv.at[j],
            device_id={"dp": partner},
            device_id_type=MESH,
        )

    for j in range(per_owner):
        core_copy(j).start()

    def back_zero(r, n, upstream, scaled_ref, slope_ref, spread_ref, hi_ref, lo_ref):
        here = pl.ds(r, n)
        back, gain_term, bias_term = norm_back(
            upstream, gain_zero, scaled_ref[here, :], spread_ref[here, :], slope_ref[here, :]
        )
        hi = back.astype(BF16)
        hi_ref[here, :] = hi
        lo_ref[here, :] = (back - hi.astype(F32)).astype(BF16)
        return fold_rows(gain_term), fold_rows(bias_term)

    def back_even(i, carry):
        r = pl.multiple_of(i * chunk_back, chunk_back)
        here = pl.ds(r, chunk_back)
        upstream = dot(back_one[here, :], w_ref[0:width, :], NT) + dot(
            back_down[here, :], w_ref[2 * width : 3 * width, :], NT
        )
        terms = back_zero(
            r, chunk_back, upstream, scaled_even, slope_even, spread_even, hi_even, lo_even
        )
        return (carry[0] + terms[0], carry[1] + terms[1])

    def back_odd(i, carry):
        r = pl.multiple_of(i * chunk_back, chunk_back)
        here = pl.ds(r, chunk_back)
        upstream = dot(back_one[here, :], w_ref[width : 2 * width, :], NT)
        terms = back_zero(
            r, chunk_back, upstream, scaled_odd, slope_odd, spread_odd, hi_odd, lo_odd
        )
        return (carry[0] + terms[0], carry[1] + terms[1])

    sums = lax.fori_loop(0, n_out // chunk_back, back_even, (zero_sum, zero_sum))
    upstream = (
        dot(back_down[n_out:n_even, :], w_ref[2 * width : 3 * width, :], NT) * keep
    )
    terms = back_zero(
        n_out, tail_rows, upstream, scaled_even, slope_even, spread_even, hi_even, lo_even
    )
    sums = (sums[0] + terms[0], sums[1] + terms[1])

    def x_copy(j, k):
        peer = lax.rem(x + k, n_x)
        return pltpu.make_async_remote_copy(
            src_ref=sum_core.at[j, pl.ds(peer * n_y, n_y)],
            dst_ref=got_x.at[j, k],
            send_sem=x_send.at[j, k],
            recv_sem=x_recv.at[j, k],
            device_id={"dp": dp_of(peer, y, core)},
            device_id_type=MESH,
        )

    order_x = sorted(range(1, n_x), key=lambda k: -min(k, n_x - k))
    for j in range(per_owner):
        core_copy(j).wait_recv()

        def add_core(i, carry):
            here = pl.ds(i * n_y, n_y)
            total = parts[j, core, here].astype(F32) + got_core[j, here].astype(F32)
            sum_core[j, here] = total.astype(BF16)
            return carry

        lax.fori_loop(0, n_x, add_core, 0)
        for k in order_x:
            x_copy(j, k).start()

    sums = lax.fori_loop(0, n_out // chunk_back, back_odd, sums)

    grad_wz = (
        dot(patches[:, 0:128], hi_even[...], TN)
        + dot(patches[:, 0:128], lo_even[...], TN)
        + dot(patches[0:n_out, 128:256], hi_odd[...], TN)
        + dot(patches[0:n_out, 128:256], lo_odd[...], TN)
    )

    def row_sum(array):
        return jnp.sum(array, axis=0, keepdims=True)

    small[0, :, :] = grad_wz[0:8]
    small[1, 0:2, :] = grad_wz[8:10]
    small[1, 2:3, :] = row_sum(sums[0])
    small[1, 3:4, :] = row_sum(sums[1])
    small[1, 4:5, :] = row_sum(sum_gain_one)
    small[1, 5:6, :] = row_sum(sum_bias_one)
    small[1, 6:8, :] = jnp.zeros((2, width), F32)
    small_core_copy = pltpu.make_async_remote_copy(
        src_ref=small.at[1 - core],
        dst_ref=small_core,
        send_sem=sc_sems.at[0],
        recv_sem=sc_sems.at[1],
        device_id={"dp": partner},
        device_id_type=MESH,
    )
    small_core_copy.start()

    def share(buffer, at, sends, recvs, axis, device):
        def copy(k):
            return pltpu.make_async_remote_copy(
                src_ref=buffer.at[at],
                dst_ref=buffer.at[at],
                send_sem=sends.at[k],
                recv_sem=recvs.at[k],
                device_id={axis: device(k)},
                device_id_type=MESH,
            )

        return copy

    sx_copy = share(
        small_x, x, sx_send, sx_recv, "dp", lambda k: dp_of(lax.rem(x + k, n_x), y, core)
    )
    sy_copy = share(small_y, y, sy_send, sy_recv, "dp", lambda k: y_peer(k)[1])
    sz_copy = share(small_z, z, sz_send, sz_recv, "seq", lambda k: lax.rem(z + k, n_z))
    z_copies = [
        share(
            got_z.at[j], z, z_send.at[j], z_recv.at[j], "seq", lambda k: lax.rem(z + k, n_z)
        )
        for j in range(per_owner)
    ]

    def total_of(buffer, count):
        total = buffer[0].astype(F32)
        for k in range(1, count):
            total = total + buffer[k].astype(F32)
        return total

    def y_copy(j, k):
        peer, device = y_peer(k)
        return pltpu.make_async_remote_copy(
            src_ref=sum_x.at[j, peer],
            dst_ref=got_y.at[j, k],
            send_sem=y_send.at[j, k],
            recv_sem=y_recv.at[j, k],
            device_id={"dp": device},
            device_id_type=MESH,
        )

    for j in range(per_owner):
        for k in range(1, n_x):
            x_copy(j, k).wait_recv()
        total = sum_core[j, pl.ds(x * n_y, n_y)].astype(F32)
        for k in range(1, n_x):
            total = total + got_x[j, k].astype(F32)
        sum_x[j] = total.astype(BF16)
        for k in order_y:
            y_copy(j, k).start()
        if j == 0:
            small_core_copy.wait_recv()
            small_x[x] = small[core] + small_core[...]
            for k in order_x:
                sx_copy(k).start()

    for k in range(1, n_x):
        sx_copy(k).wait_recv()
    small_y[y] = total_of(small_x, n_x)
    for k in order_y:
        sy_copy(k).start()

    for j in range(per_owner):
        if j == per_owner - 1:
            for k in range(1, n_y):
                sy_copy(k).wait_recv()
            small_z[z] = total_of(small_y, n_y).astype(BF16)
            for k in order_z:
                sz_copy(k).start()
        for k in range(1, n_y):
            y_copy(j, k).wait_recv()
        total = sum_x[j, y].astype(F32)
        for k in range(1, n_y):
            total = total + got_y[j, k].astype(F32)
        got_z[j, z] = total.astype(BF16)
        for k in order_z:
            z_copies[j](k).start()

    def finish(j):
        for k in range(1, n_z):
            z_copies[j](k).wait_recv()
        grad_ref[8 * j : 8 * j + 8, :] = total_of(got_z.at[j], n_z)

    for j in range(per_owner - 1):
        finish(j)
    for k in range(1, n_z):
        sz_copy(k).wait_recv()
    total = total_of(small_z, n_z)
    small_half[...] = total
    full_copy = pltpu.make_async_remote_copy(
        src_ref=small_half,
        dst_ref=small_full.at[core],
        send_sem=sf_sems.at[0],
        recv_sem=sf_sems.at[1],
        device_id={"dp": partner},
        device_id_type=MESH,
    )
    full_copy.start()
    small_full[core] = total
    finish(per_owner - 1)
    full_copy.wait_recv()

    keep_feats.wait()
    rim_copy.wait_send()
    small_core_copy.wait_send()
    full_copy.wait_send()
    for k in range(1, n_near):
        near_copy(k).wait_send()
    for k in range(1, n_x):
        sx_copy(k).wait_send()
    for k in range(1, n_y):
        far_copy(k).wait_send()
        sy_copy(k).wait_send()
    for k in range(1, n_z):
        sz_copy(k).wait_send()
    for j in range(per_owner):
        core_copy(j).wait_send()
        for k in range(1, n_x):
            x_copy(j, k).wait_send()
        for k in range(1, n_y):
            y_copy(j, k).wait_send()
        for k in range(1, n_z):
            z_copies[j](k).wait_send()


def hand_out(
    feats_in, grad_in, small_ref, feats_ref, grad_ref, gwz_ref, ggz_ref, gbz_ref, gg1_ref, gb1_ref
):
    feats_ref[...] = feats_in[...]
    grad_ref[...] = grad_in[...]
    gwz_ref[0:8, :] = small_ref[0]
    rest = small_ref[1]
    gwz_ref[8:10, :] = rest[0:2]
    ggz_ref[...] = rest[2:3]
    gbz_ref[...] = rest[3:4]
    gg1_ref[...] = rest[4:5]
    gb1_ref[...] = rest[5:6]


def on_device(n_dp, n_z, audio, send, place, cot, conv_zero, conv_one, gz, bz, g1, b1):
    n_x = n_dp // (n_core * n_y)
    n_rows, n_out, width = audio.shape[1], cot.shape[1], cot.shape[2]
    n_even = n_out + tail_rows
    per_owner = 3 * width // 8 // n_dp
    n_near = n_x * n_core
    vmem = lambda *shape, dtype=F32: pltpu.VMEM(shape, dtype)
    page = lambda *shape: pltpu.VMEM((*shape, 8, width), BF16)
    dma = lambda *shape: pltpu.SemaphoreType.DMA(shape)
    scratch = [
        vmem(n_out, width, dtype=BF16),
        vmem(3 * width, width, dtype=BF16),
        vmem(n_out, width, dtype=BF16),
        vmem(n_near, n_y, 1, lanes),
        vmem(n_near, n_y, 1, lanes),
        vmem(n_y, n_near, 1, lanes),
        vmem(8, lanes),
        vmem(8, lanes),
        vmem(n_rows + 8, lanes),
        vmem(n_even, lanes, dtype=BF16),
        vmem(128, width, dtype=BF16),
        vmem(n_even, width, dtype=BF16),
        vmem(n_out, width, dtype=BF16),
        vmem(n_even, width),
        vmem(n_out, width),
        vmem(n_even, width),
        vmem(n_out, width),
        vmem(n_even, 1),
        vmem(n_out, 1),
        vmem(n_even, width),
        vmem(n_out, width, dtype=BF16),
        vmem(n_out + 32, width),
        vmem(n_even, width, dtype=BF16),
        vmem(n_even, width, dtype=BF16),
        vmem(n_even, width, dtype=BF16),
        vmem(n_out, width, dtype=BF16),
        vmem(n_out, width, dtype=BF16),
        page(per_owner, n_core, n_x * n_y),
        page(per_owner, n_x * n_y),
        page(per_owner, n_x * n_y),
        page(per_owner, n_x, n_y),
        page(per_owner, n_y),
        page(per_owner, n_y),
        page(per_owner, n_z),
        vmem(2, 8, width),
        vmem(8, width),
        vmem(n_x, 8, width),
        vmem(n_y, 8, width),
        page(n_z),
        vmem(8, width),
        dma(3),
        dma(n_near),
        dma(n_near),
        dma(n_y),
        dma(n_y),
        dma(2),
        dma(per_owner),
        dma(per_owner),
        dma(per_owner, n_x),
        dma(per_owner, n_x),
        dma(per_owner, n_y),
        dma(per_owner, n_y),
        dma(per_owner, n_z),
        dma(per_owner, n_z),
        dma(2),
        dma(n_x),
        dma(n_x),
        dma(n_y),
        dma(n_y),
        dma(n_z),
        dma(n_z),
        dma(2),
    ]
    row = jax.ShapeDtypeStruct((1, width), F32)
    in_vmem = pl.BlockSpec(memory_space=pltpu.VMEM)
    anywhere = pl.BlockSpec(memory_space=pl.ANY)
    feats, grad, small = pl.pallas_call(
        functools.partial(kernel, (n_dp, n_x, n_z, n_rows, n_out, width)),
        out_shape=(
            jax.ShapeDtypeStruct((n_out, width), BF16),
            jax.ShapeDtypeStruct((3 * width // n_dp, width), F32),
            jax.ShapeDtypeStruct((2, 8, width), F32),
        ),
        in_specs=[in_vmem, in_vmem, in_vmem, anywhere, in_vmem, anywhere, *[in_vmem] * 4],
        out_specs=(anywhere, in_vmem, in_vmem),
        scratch_shapes=scratch,
        compiler_params=pltpu.CompilerParams(
            collective_id=0, has_side_effects=True, vmem_limit_bytes=60 * 2**20
        ),
    )(
        audio[0].T,
        send.reshape(1, -1),
        place.reshape(1, -1),
        cot[0],
        conv_zero,
        conv_one,
        gz[None],
        bz[None],
        g1[None],
        b1[None],
    )
    feats, grad, gwz, ggz, gbz, gg1, gb1 = pl.pallas_call(
        hand_out,
        out_shape=(
            jax.ShapeDtypeStruct(feats.shape, feats.dtype),
            jax.ShapeDtypeStruct(grad.shape, grad.dtype),
            jax.ShapeDtypeStruct((10, width), F32),
            row,
            row,
            row,
            row,
        ),
        in_specs=[in_vmem] * 3,
        out_specs=(in_vmem,) * 7,
        compiler_params=pltpu.CompilerParams(vmem_limit_bytes=60 * 2**20),
    )(feats, grad, small)
    return feats[None], grad, gwz, ggz[0], gbz[0], gg1[0], gb1[0]


def solution(mesh):
    placed = (
        P("dp", "seq", None),
        P("seq", "dp", None),
        P("seq", "dp", None),
        P("dp", "seq", None),
        P(),
        P(),
        P(),
        P(),
        P(),
        P(),
    )
    return jax.shard_map(
        functools.partial(on_device, mesh.shape["dp"], mesh.shape["seq"]),
        mesh=mesh,
        in_specs=placed,
        out_specs=(P("dp", "seq", None), P("dp", None), P(), P(), P(), P(), P()),
        check_vma=False,
    )
```

```python
import functools

import jax
import jax.numpy as jnp
from jax import lax
from jax.experimental import pallas as pl
from jax.experimental.pallas import tpu as pltpu
from jax.sharding import PartitionSpec as P

MESH = pl.DeviceIdType.MESH
F32 = jnp.float32
BF16 = jnp.bfloat16
norm_eps = 1e-05
n_core = 2
n_y = 8
slots = 4
group = 64
lanes = slots * group
chunk_zero = 128
chunk_one = 128
chunk_back = 128
tail_rows = 16
quarters = 4


def iota(shape, dim):
    return lax.broadcasted_iota(jnp.int32, shape, dim)


def one_hot(mask):
    return jnp.where(mask, 1.0, 0.0).astype(BF16)


def dot(a, b, dims=((1,), (0,))):
    return lax.dot_general(a, b, (dims, ((), ())), preferred_element_type=F32)


TN = ((0,), (0,))
NT = ((1,), (1,))


def norm_gelu(pre, gain, bias):
    center = pre - jnp.mean(pre, axis=-1, keepdims=True)
    spread = lax.rsqrt(jnp.mean(center * center, axis=-1, keepdims=True) + norm_eps)
    scaled = center * spread
    normed = scaled * gain + bias
    below = 0.5 + 0.5 * lax.erf(normed * 0.7071067811865476)
    act = normed * below
    slope = below + normed * (jnp.exp(-0.5 * normed * normed) * 0.3989422804014327)
    return act, scaled, spread, slope


def norm_back(upstream, gain, scaled, spread, slope):
    inner = upstream * slope
    pushed = inner * gain
    back = spread * (
        pushed
        - jnp.mean(pushed, axis=-1, keepdims=True)
        - scaled * jnp.mean(pushed * scaled, axis=-1, keepdims=True)
    )
    return back, inner * scaled, inner


def fold_rows(array):
    return jnp.sum(array.reshape(array.shape[0] // 8, 8, array.shape[1]), axis=0)


def kernel(
    sizes,
    audio_ref,
    send_ref,
    place_ref,
    cot_hbm,
    wz_ref,
    w_hbm,
    gz_ref,
    bz_ref,
    g1_ref,
    b1_ref,
    feats_hbm,
    grad_ref,
    small_full,
    cot_ref,
    w_ref,
    feats_ref,
    msg,
    got_msg,
    arr,
    own_row,
    rim,
    samples,
    patches,
    wz_pad,
    act_even,
    act_odd,
    scaled_even,
    scaled_odd,
    slope_even,
    slope_odd,
    spread_even,
    spread_odd,
    third,
    back_one,
    back_f32,
    back_down,
    hi_even,
    lo_even,
    hi_odd,
    lo_odd,
    parts,
    got_core,
    sum_core,
    got_x,
    sum_x,
    got_y,
    got_y_first,
    sum_y_first,
    got_x_second,
    got_z,
    small,
    small_core,
    small_x,
    small_y,
    small_z,
    small_half,
    load_sems,
    near_send,
    near_recv,
    far_send,
    far_recv,
    rim_sems,
    core_send,
    core_recv,
    x_send,
    x_recv,
    y_send,
    y_recv,
    z_send,
    z_recv,
    sc_sems,
    sx_send,
    sx_recv,
    sy_send,
    sy_recv,
    sz_send,
    sz_recv,
    sf_sems,
):
    n_dp, n_x, n_z, n_rows, n_out, width = sizes
    n_even = n_out + tail_rows
    me = lax.axis_index("dp")
    z = lax.axis_index("seq")
    core = lax.rem(me, n_core)
    y = lax.rem(me // n_core, n_y)
    x = me // (n_core * n_y)

    def dp_of(px, py, pc):
        return (px * n_y + py) * n_core + pc

    n_near = n_x * n_core
    near = x * n_core + core

    def near_peer(k):
        at = lax.rem(near + k, n_near)
        return at, dp_of(at // n_core, y, lax.rem(at, n_core))

    def y_peer(k):
        at = lax.rem(y + k, n_y)
        return at, dp_of(x, at, core)

    barrier = pltpu.get_barrier_semaphore()

    def greet(axis, device):
        pl.semaphore_signal(barrier, inc=1, device_id={axis: device}, device_id_type=MESH)

    for k in range(1, n_near):
        greet("dp", near_peer(k)[1])
    for k in range(1, n_y):
        greet("dp", y_peer(k)[1])
    for k in range(1, n_z):
        greet("seq", lax.rem(z + k, n_z))

    load_w = pltpu.make_async_copy(w_hbm, w_ref, load_sems.at[0])
    load_cot = pltpu.make_async_copy(cot_hbm, cot_ref, load_sems.at[1])
    load_w.start()
    load_cot.start()

    spread_lanes = one_hot(
        jnp.bitwise_and(iota((40, lanes), 1), group - 1) == iota((40, lanes), 0)
    )
    blocks = dot(audio_ref[...], spread_lanes, TN).astype(BF16)
    chosen = one_hot(iota((n_rows, n_dp * slots), 0) == send_ref[...])
    picked = dot(chosen, blocks, TN)
    slot_of = jnp.bitwise_and(iota((n_dp * slots, lanes), 0), slots - 1)
    lane_group = lax.shift_right_logical(iota((n_dp * slots, lanes), 1), 6)
    in_group = slot_of == lane_group
    picked = jnp.where(in_group, picked, 0.0).astype(BF16)
    bit_y = n_y.bit_length() - 1

    def of_slot(shape, dim):
        device = lax.shift_right_logical(iota(shape, dim), 2)
        at_core = jnp.bitwise_and(device, n_core - 1)
        at_y = jnp.bitwise_and(lax.shift_right_logical(device, 1), n_y - 1)
        return lax.shift_right_logical(device, 1 + bit_y) * n_core + at_core, at_y

    slot_near, slot_y = of_slot((n_dp, n_dp * slots), 1)
    gather_dest = one_hot(slot_near * n_y + slot_y == iota((n_dp, n_dp * slots), 0))
    message = dot(gather_dest, picked)
    for d in range(n_dp):
        msg[d // n_y, d % n_y] = message[d : d + 1]

    pl.semaphore_wait(barrier, n_near - 1 + n_y - 1 + n_z - 1)

    def near_copy(k):
        at, device = near_peer(k)
        return pltpu.make_async_remote_copy(
            src_ref=msg.at[at],
            dst_ref=got_msg.at[near],
            send_sem=near_send.at[k],
            recv_sem=near_recv.at[k],
            device_id={"dp": device},
            device_id_type=MESH,
        )

    for k in range(1, n_near):
        near_copy(k).start()
    got_msg[near] = msg[near]

    wz_pad[...] = jnp.zeros_like(wz_pad)
    wz_pad[0:10, :] = wz_ref[...]
    gain_zero, bias_zero = gz_ref[...], bz_ref[...]
    gain_one, bias_one = g1_ref[...], b1_ref[...]
    keep = jnp.where(z < n_z - 1, 1.0, 0.0).astype(F32)
    placed = one_hot(iota((n_dp * slots, n_rows), 0) == place_ref[...])
    slot_near, slot_y = of_slot((n_dp * slots, n_dp), 0)
    spread_slots = one_hot(slot_y * n_near + slot_near == iota((n_dp * slots, n_dp), 1))
    lane_in, lane_out = iota((lanes, lanes), 0), iota((lanes, lanes), 1)
    sample_in = jnp.bitwise_and(lane_in, group - 1)
    sample_out = jnp.bitwise_and(lane_out, group - 1)
    fold_here = one_hot((sample_in == sample_out) & (sample_out < 40))
    fold_next = one_hot((sample_in + 40 == sample_out) & (sample_out < 45))
    row_id = iota((n_out, n_rows), 0)
    widen = one_hot(lax.shift_right_logical(row_id, 2) == iota((n_out, n_rows), 1))
    phase = jnp.bitwise_and(iota((n_out, lanes), 0), 3)
    own_phase = phase == lax.shift_right_logical(iota((n_out, lanes), 1), 6)
    tap = sample_in - 10 * lax.shift_right_logical(lane_in, 6)
    wanted = jnp.where(lane_out < 128, lane_out, lane_out - 128 + 5)
    limit = jnp.where(lane_out < 128, 10, 15)
    to_patch = one_hot((tap == wanted) & (wanted < limit))
    edge_from = jnp.where(lane_out < 128, lane_out, lane_out - 133)
    edge_limit = jnp.where(lane_out < 128, 10, 5)
    to_edge = one_hot((sample_in == edge_from) & (edge_from < edge_limit))

    for k in range(1, n_near):
        near_copy(k).wait_recv()

    def far_copy(k):
        at, device = y_peer(k)
        return pltpu.make_async_remote_copy(
            src_ref=got_msg.at[:, at],
            dst_ref=arr.at[y],
            send_sem=far_send.at[k],
            recv_sem=far_recv.at[k],
            device_id={"dp": device},
            device_id_type=MESH,
        )

    order_y = sorted(range(1, n_y), key=lambda k: -min(k, n_y - k))
    order_z = sorted(range(1, n_z), key=lambda k: -min(k, n_z - k))
    for k in order_y:
        far_copy(k).start()
    arr[y] = got_msg[:, y]
    for k in range(1, n_y):
        far_copy(k).wait_recv()

    received = jnp.concatenate(
        [arr[s // n_near, s % n_near] for s in range(n_dp)], axis=0
    ).astype(BF16)
    by_slot = dot(spread_slots, received)
    by_slot = jnp.where(in_group, by_slot, 0.0).astype(BF16)
    ordered = dot(placed, by_slot, TN)
    own_row[...] = dot(ordered[0:8].astype(BF16), to_edge)
    rim_copy = pltpu.make_async_remote_copy(
        src_ref=own_row,
        dst_ref=rim,
        send_sem=rim_sems.at[0],
        recv_sem=rim_sems.at[1],
        device_id={"seq": lax.rem(z + n_z - 1, n_z)},
        device_id_type=MESH,
    )
    rim_copy.start()
    samples[0:n_rows, :] = ordered
    samples[n_rows : n_rows + 8, :] = jnp.zeros((8, lanes), F32)
    wide = dot(samples[0:n_rows, :].astype(BF16), fold_here) + dot(
        samples[1 : n_rows + 1, :].astype(BF16), fold_next
    )
    rows = dot(widen, wide.astype(BF16))
    rows = jnp.where(own_phase, rows, 0.0).astype(BF16)
    patches[0:n_out, :] = dot(rows, to_patch).astype(BF16)

    def forward_even(r, n):
        pre = dot(patches[pl.ds(r, n), 0:128], wz_pad[...])
        act, scaled, spread, slope = norm_gelu(pre, gain_zero, bias_zero)
        scaled_even[pl.ds(r, n), :] = scaled
        slope_even[pl.ds(r, n), :] = slope
        spread_even[pl.ds(r, n), :] = spread
        return act

    def forward_odd(r, n):
        pre = dot(patches[pl.ds(r, n), 128:256], wz_pad[...])
        act, scaled, spread, slope = norm_gelu(pre, gain_zero, bias_zero)
        act_odd[pl.ds(r, n), :] = act.astype(BF16)
        scaled_odd[pl.ds(r, n), :] = scaled
        slope_odd[pl.ds(r, n), :] = slope
        spread_odd[pl.ds(r, n), :] = spread

    def forward_zero(i, carry):
        r = pl.multiple_of(i * chunk_zero, chunk_zero)
        act_even[pl.ds(r, chunk_zero), :] = forward_even(r, chunk_zero).astype(BF16)
        forward_odd(r, chunk_zero)
        return carry

    lax.fori_loop(0, n_out // chunk_zero, forward_zero, 0)

    rim_copy.wait_recv()
    edge = rim[0:1, :] * keep
    tail_id = iota((tail_rows, 128), 0)
    last = pl.ds(n_out - tail_rows, tail_rows)
    patches[last, 128:256] = (
        patches[last, 128:256].astype(F32)
        + jnp.where(tail_id == tail_rows - 1, edge[:, 128:256], 0.0)
    ).astype(BF16)
    patches[n_out:n_even, 0:128] = jnp.where(tail_id == 0, edge[:, 0:128], 0.0).astype(BF16)
    forward_odd(n_out - tail_rows, tail_rows)
    act_even[n_out:n_even, :] = (forward_even(n_out, tail_rows) * keep).astype(BF16)
    load_w.wait()

    third[...] = dot(act_even[...], w_ref[2 * width : 3 * width, :])
    for r in range(0, n_out, 64):
        third[r : r + 64, :] = third[r + 1 : r + 65, :]
    load_cot.wait()

    def layer_one(i, carry):
        sum_gain, sum_bias = carry
        r = pl.multiple_of(i * chunk_one, chunk_one)
        here = pl.ds(r, chunk_one)
        pre = (
            dot(act_even[here, :], w_ref[0:width, :])
            + dot(act_odd[here, :], w_ref[width : 2 * width, :])
            + third[here, :]
        )
        act, scaled, spread, slope = norm_gelu(pre, gain_one, bias_one)
        feats_ref[here, :] = act.astype(BF16)
        back, gain_term, bias_term = norm_back(
            cot_ref[here, :].astype(F32), gain_one, scaled, spread, slope
        )
        back = back.astype(BF16)
        back_one[here, :] = back
        back_f32[pl.ds(r + 8, chunk_one), :] = back.astype(F32)
        return (sum_gain + fold_rows(gain_term), sum_bias + fold_rows(bias_term))

    zero_sum = jnp.zeros((8, width), F32)
    back_f32[0:8, :] = jnp.zeros((8, width), F32)
    back_f32[n_out + 8 :, :] = jnp.zeros((back_f32.shape[0] - n_out - 8, width), F32)
    sum_gain_one, sum_bias_one = lax.fori_loop(
        0, n_out // chunk_one, layer_one, (zero_sum, zero_sum)
    )
    back_down[...] = back_f32[7 : 7 + n_even, :].astype(BF16)

    keep_feats = pltpu.make_async_copy(feats_ref, feats_hbm, load_sems.at[2])
    keep_feats.start()

    per_owner = 3 * width // 8 // n_dp
    cols = width // quarters
    partner = dp_of(x, y, 1 - core)

    def keep_pages(first_page, quarter, value):
        for i in range(width // 8):
            page = first_page + i
            d, j = page // per_owner, page % per_owner
            px, py, pc = d // (n_core * n_y), (d // n_core) % n_y, d % n_core
            for q in range(2):
                parts[quarter + q, pc, px, py, j] = value[
                    8 * i : 8 * i + 8, q * cols : (q + 1) * cols
                ].astype(BF16)

    def core_copy(q):
        return pltpu.make_async_remote_copy(
            src_ref=parts.at[q, 1 - core],
            dst_ref=got_core.at[q],
            send_sem=core_send.at[q],
            recv_sem=core_recv.at[q],
            device_id={"dp": partner},
            device_id_type=MESH,
        )

    for q in range(0, quarters, 2):
        here = slice(q * cols, (q + 2) * cols)
        keep_pages(0, q, dot(act_even[0:n_out, :], back_one[:, here], TN))
        keep_pages(width // 8, q, dot(act_odd[...], back_one[:, here], TN))
        keep_pages(2 * width // 8, q, dot(act_even[...], back_down[:, here], TN))
        core_copy(q).start()
        core_copy(q + 1).start()

    def back_zero(r, n, upstream, scaled_ref, slope_ref, spread_ref, hi_ref, lo_ref):
        here = pl.ds(r, n)
        back, gain_term, bias_term = norm_back(
            upstream, gain_zero, scaled_ref[here, :], spread_ref[here, :], slope_ref[here, :]
        )
        hi = back.astype(BF16)
        hi_ref[here, :] = hi
        lo_ref[here, :] = (back - hi.astype(F32)).astype(BF16)
        return fold_rows(gain_term), fold_rows(bias_term)

    def back_even(i, carry):
        r = pl.multiple_of(i * chunk_back, chunk_back)
        here = pl.ds(r, chunk_back)
        upstream = dot(back_one[here, :], w_ref[0:width, :], NT) + dot(
            back_down[here, :], w_ref[2 * width : 3 * width, :], NT
        )
        terms = back_zero(
            r, chunk_back, upstream, scaled_even, slope_even, spread_even, hi_even, lo_even
        )
        return (carry[0] + terms[0], carry[1] + terms[1])

    def back_odd(i, carry):
        r = pl.multiple_of(i * chunk_back, chunk_back)
        here = pl.ds(r, chunk_back)
        upstream = dot(back_one[here, :], w_ref[width : 2 * width, :], NT)
        terms = back_zero(
            r, chunk_back, upstream, scaled_odd, slope_odd, spread_odd, hi_odd, lo_odd
        )
        return (carry[0] + terms[0], carry[1] + terms[1])

    order_x = sorted(range(1, n_x), key=lambda k: -min(k, n_x - k))

    def x_peer(k):
        at = lax.rem(x + k, n_x)
        return at, dp_of(at, y, core)

    def send(src, dst, send_sem, recv_sem, axis, device):
        return pltpu.make_async_remote_copy(
            src_ref=src,
            dst_ref=dst,
            send_sem=send_sem,
            recv_sem=recv_sem,
            device_id={axis: device},
            device_id_type=MESH,
        )

    def x_copy(q, k):
        at, device = x_peer(k)
        src, dst = (
            (sum_y_first.at[at], got_x_second.at[k])
            if q == 0
            else (sum_core.at[q, at], got_x.at[q, k])
        )
        return send(src, dst, x_send.at[q, k], x_recv.at[q, k], "dp", device)

    def y_copy(q, k):
        at, device = y_peer(k)
        src, dst = (
            (sum_core.at[0, :, at], got_y_first.at[k])
            if q == 0
            else (sum_x.at[q, at], got_y.at[q, k])
        )
        return send(src, dst, y_send.at[q, k], y_recv.at[q, k], "dp", device)

    def pair_sum(q):
        core_copy(q).wait_recv()

        def add_core(i, carry):
            total = parts[q, core, i].astype(F32) + got_core[q, i].astype(F32)
            sum_core[q, i] = total.astype(BF16)
            return carry

        lax.fori_loop(0, n_x, add_core, 0)
        if q == 0:
            for k in order_y:
                y_copy(0, k).start()
        else:
            for k in order_x:
                x_copy(q, k).start()

    sums = back_even(0, (zero_sum, zero_sum))
    pair_sum(0)
    pair_sum(1)
    n_chunks = n_out // chunk_back
    if n_chunks > 1:
        sums = back_even(1, sums)
    pair_sum(2)
    pair_sum(3)
    for i in range(2, n_chunks):
        sums = back_even(i, sums)
    upstream = (
        dot(back_down[n_out:n_even, :], w_ref[2 * width : 3 * width, :], NT) * keep
    )
    terms = back_zero(
        n_out, tail_rows, upstream, scaled_even, slope_even, spread_even, hi_even, lo_even
    )
    sums = (sums[0] + terms[0], sums[1] + terms[1])
    sums = lax.fori_loop(0, n_chunks, back_odd, sums)

    grad_wz = (
        dot(patches[:, 0:128], hi_even[...], TN)
        + dot(patches[:, 0:128], lo_even[...], TN)
        + dot(patches[0:n_out, 128:256], hi_odd[...], TN)
        + dot(patches[0:n_out, 128:256], lo_odd[...], TN)
    )

    def row_sum(array):
        return jnp.sum(array, axis=0, keepdims=True)

    small[0, :, :] = grad_wz[0:8]
    small[1, 0:2, :] = grad_wz[8:10]
    small[1, 2:3, :] = row_sum(sums[0])
    small[1, 3:4, :] = row_sum(sums[1])
    small[1, 4:5, :] = row_sum(sum_gain_one)
    small[1, 5:6, :] = row_sum(sum_bias_one)
    small[1, 6:8, :] = jnp.zeros((2, width), F32)
    small_core_copy = pltpu.make_async_remote_copy(
        src_ref=small.at[1 - core],
        dst_ref=small_core,
        send_sem=sc_sems.at[0],
        recv_sem=sc_sems.at[1],
        device_id={"dp": partner},
        device_id_type=MESH,
    )
    small_core_copy.start()

    def share(buffer, at, sends, recvs, axis, device):
        def copy(k):
            return pltpu.make_async_remote_copy(
                src_ref=buffer.at[at],
                dst_ref=buffer.at[at],
                send_sem=sends.at[k],
                recv_sem=recvs.at[k],
                device_id={axis: device(k)},
                device_id_type=MESH,
            )

        return copy

    sx_copy = share(small_x, x, sx_send, sx_recv, "dp", lambda k: x_peer(k)[1])
    sy_copy = share(small_y, y, sy_send, sy_recv, "dp", lambda k: y_peer(k)[1])
    sz_copy = share(small_z, z, sz_send, sz_recv, "seq", lambda k: lax.rem(z + k, n_z))
    z_copies = [
        share(
            got_z.at[q], z, z_send.at[q], z_recv.at[q], "seq", lambda k: lax.rem(z + k, n_z)
        )
        for q in range(quarters)
    ]

    def total_of(buffer, count):
        total = buffer[0].astype(F32)
        for k in range(1, count):
            total = total + buffer[k].astype(F32)
        return total

    def plus_got(total, buffer, count):
        total = total.astype(F32)
        for k in range(1, count):
            total = total + buffer[k].astype(F32)
        return total.astype(BF16)

    def got_all(copy, count):
        for k in range(1, count):
            copy(k).wait_recv()

    def along_y(q):
        got_all(functools.partial(x_copy, q), n_x)
        sum_x[q] = plus_got(sum_core[q, x], got_x.at[q], n_x)
        for k in order_y:
            y_copy(q, k).start()

    def along_z(q):
        if q == 0:
            got_all(functools.partial(x_copy, 0), n_x)
            got_z[0, z] = plus_got(sum_y_first[x], got_x_second, n_x)
        else:
            got_all(functools.partial(y_copy, q), n_y)
            got_z[q, z] = plus_got(sum_x[q, y], got_y.at[q], n_y)
        for k in order_z:
            z_copies[q](k).start()

    def finish(q):
        got_all(z_copies[q], n_z)
        total = total_of(got_z.at[q], n_z)
        for j in range(per_owner):
            grad_ref[8 * j : 8 * j + 8, q * cols : (q + 1) * cols] = total[j]

    along_y(1)
    small_core_copy.wait_recv()
    small_z[z] = (small[core] + small_core[...]).astype(BF16)
    for k in order_z:
        sz_copy(k).start()
    along_y(2)
    got_all(functools.partial(y_copy, 0), n_y)
    sum_y_first[...] = plus_got(sum_core[0, :, y], got_y_first, n_y)
    for k in order_x:
        x_copy(0, k).start()
    along_y(3)
    along_z(1)
    along_z(0)
    got_all(sz_copy, n_z)
    small_x[x] = total_of(small_z, n_z)
    for k in order_x:
        sx_copy(k).start()
    along_z(2)
    got_all(sx_copy, n_x)
    small_y[y] = total_of(small_x, n_x)
    for k in order_y:
        sy_copy(k).start()
    along_z(3)
    finish(1)
    finish(0)
    got_all(sy_copy, n_y)
    total = total_of(small_y, n_y)
    small_half[...] = total
    full_copy = send(
        small_half, small_full.at[core], sf_sems.at[0], sf_sems.at[1], "dp", partner
    )
    full_copy.start()
    small_full[core] = total
    finish(2)
    finish(3)
    full_copy.wait_recv()

    keep_feats.wait()
    rim_copy.wait_send()
    small_core_copy.wait_send()
    full_copy.wait_send()
    for k in range(1, n_near):
        near_copy(k).wait_send()
    for k in range(1, n_x):
        sx_copy(k).wait_send()
    for k in range(1, n_y):
        far_copy(k).wait_send()
        sy_copy(k).wait_send()
    for k in range(1, n_z):
        sz_copy(k).wait_send()
    for q in range(quarters):
        core_copy(q).wait_send()
        for k in range(1, n_x):
            x_copy(q, k).wait_send()
        for k in range(1, n_y):
            y_copy(q, k).wait_send()
        for k in range(1, n_z):
            z_copies[q](k).wait_send()


def hand_out(
    feats_in, grad_in, small_ref, feats_ref, grad_ref, gwz_ref, ggz_ref, gbz_ref, gg1_ref, gb1_ref
):
    feats_ref[...] = feats_in[...]
    grad_ref[...] = grad_in[...]
    gwz_ref[0:8, :] = small_ref[0]
    rest = small_ref[1]
    gwz_ref[8:10, :] = rest[0:2]
    ggz_ref[...] = rest[2:3]
    gbz_ref[...] = rest[3:4]
    gg1_ref[...] = rest[4:5]
    gb1_ref[...] = rest[5:6]


def on_device(n_dp, n_z, audio, send, place, cot, conv_zero, conv_one, gz, bz, g1, b1):
    n_x = n_dp // (n_core * n_y)
    n_rows, n_out, width = audio.shape[1], cot.shape[1], cot.shape[2]
    n_even = n_out + tail_rows
    per_owner = 3 * width // 8 // n_dp
    n_near = n_x * n_core
    vmem = lambda *shape, dtype=F32: pltpu.VMEM(shape, dtype)
    page = lambda *shape: pltpu.VMEM((*shape, per_owner, 8, width // quarters), BF16)
    dma = lambda *shape: pltpu.SemaphoreType.DMA(shape)
    scratch = [
        vmem(n_out, width, dtype=BF16),
        vmem(3 * width, width, dtype=BF16),
        vmem(n_out, width, dtype=BF16),
        vmem(n_near, n_y, 1, lanes),
        vmem(n_near, n_y, 1, lanes),
        vmem(n_y, n_near, 1, lanes),
        vmem(8, lanes),
        vmem(8, lanes),
        vmem(n_rows + 8, lanes),
        vmem(n_even, lanes, dtype=BF16),
        vmem(128, width, dtype=BF16),
        vmem(n_even, width, dtype=BF16),
        vmem(n_out, width, dtype=BF16),
        vmem(n_even, width),
        vmem(n_out, width),
        vmem(n_even, width),
        vmem(n_out, width),
        vmem(n_even, 1),
        vmem(n_out, 1),
        vmem(n_even, width),
        vmem(n_out, width, dtype=BF16),
        vmem(n_out + 32, width),
        vmem(n_even, width, dtype=BF16),
        vmem(n_even, width, dtype=BF16),
        vmem(n_even, width, dtype=BF16),
        vmem(n_out, width, dtype=BF16),
        vmem(n_out, width, dtype=BF16),
        page(quarters, n_core, n_x, n_y),
        page(quarters, n_x, n_y),
        page(quarters, n_x, n_y),
        page(quarters, n_x, n_y),
        page(quarters, n_y),
        page(quarters, n_y),
        page(n_y, n_x),
        page(n_x),
        page(n_x),
        page(quarters, n_z),
        vmem(2, 8, width),
        vmem(8, width),
        vmem(n_x, 8, width),
        vmem(n_y, 8, width),
        vmem(n_z, 8, width, dtype=BF16),
        vmem(8, width),
        dma(3),
        dma(n_near),
        dma(n_near),
        dma(n_y),
        dma(n_y),
        dma(2),
        dma(quarters),
        dma(quarters),
        dma(quarters, n_x),
        dma(quarters, n_x),
        dma(quarters, n_y),
        dma(quarters, n_y),
        dma(quarters, n_z),
        dma(quarters, n_z),
        dma(2),
        dma(n_x),
        dma(n_x),
        dma(n_y),
        dma(n_y),
        dma(n_z),
        dma(n_z),
        dma(2),
    ]
    row = jax.ShapeDtypeStruct((1, width), F32)
    in_vmem = pl.BlockSpec(memory_space=pltpu.VMEM)
    anywhere = pl.BlockSpec(memory_space=pl.ANY)
    feats, grad, small = pl.pallas_call(
        functools.partial(kernel, (n_dp, n_x, n_z, n_rows, n_out, width)),
        out_shape=(
            jax.ShapeDtypeStruct((n_out, width), BF16),
            jax.ShapeDtypeStruct((3 * width // n_dp, width), F32),
            jax.ShapeDtypeStruct((2, 8, width), F32),
        ),
        in_specs=[in_vmem, in_vmem, in_vmem, anywhere, in_vmem, anywhere, *[in_vmem] * 4],
        out_specs=(anywhere, in_vmem, in_vmem),
        scratch_shapes=scratch,
        compiler_params=pltpu.CompilerParams(
            collective_id=0, has_side_effects=True, vmem_limit_bytes=60 * 2**20
        ),
    )(
        audio[0].T,
        send.reshape(1, -1),
        place.reshape(1, -1),
        cot[0],
        conv_zero,
        conv_one,
        gz[None],
        bz[None],
        g1[None],
        b1[None],
    )
    feats, grad, gwz, ggz, gbz, gg1, gb1 = pl.pallas_call(
        hand_out,
        out_shape=(
            jax.ShapeDtypeStruct(feats.shape, feats.dtype),
            jax.ShapeDtypeStruct(grad.shape, grad.dtype),
            jax.ShapeDtypeStruct((10, width), F32),
            row,
            row,
            row,
            row,
        ),
        in_specs=[in_vmem] * 3,
        out_specs=(in_vmem,) * 7,
        compiler_params=pltpu.CompilerParams(vmem_limit_bytes=60 * 2**20),
    )(feats, grad, small)
    return feats[None], grad, gwz, ggz[0], gbz[0], gg1[0], gb1[0]


def solution(mesh):
    placed = (
        P("dp", "seq", None),
        P("seq", "dp", None),
        P("seq", "dp", None),
        P("dp", "seq", None),
        P(),
        P(),
        P(),
        P(),
        P(),
        P(),
    )
    return jax.shard_map(
        functools.partial(on_device, mesh.shape["dp"], mesh.shape["seq"]),
        mesh=mesh,
        in_specs=placed,
        out_specs=(P("dp", "seq", None), P("dp", None), P(), P(), P(), P(), P()),
        check_vma=False,
    )
```

```python
import functools

import jax
import jax.numpy as jnp
from jax import lax
from jax.experimental import pallas as pl
from jax.experimental.pallas import tpu as pltpu
from jax.sharding import PartitionSpec as P

MESH = pl.DeviceIdType.MESH
F32 = jnp.float32
BF16 = jnp.bfloat16
norm_eps = 1e-05
n_core = 2
n_y = 8
slots = 4
group = 64
lanes = slots * group
chunk_zero = 128
chunk_one = 128
chunk_back = 128
tail_rows = 16
quarters = 4


def iota(shape, dim):
    return lax.broadcasted_iota(jnp.int32, shape, dim)


def one_hot(mask):
    return jnp.where(mask, 1.0, 0.0).astype(BF16)


def dot(a, b, dims=((1,), (0,))):
    return lax.dot_general(a, b, (dims, ((), ())), preferred_element_type=F32)


TN = ((0,), (0,))
NT = ((1,), (1,))


def norm_gelu(pre, gain, bias):
    center = pre - jnp.mean(pre, axis=-1, keepdims=True)
    spread = lax.rsqrt(jnp.mean(center * center, axis=-1, keepdims=True) + norm_eps)
    scaled = center * spread
    normed = scaled * gain + bias
    below = 0.5 + 0.5 * lax.erf(normed * 0.7071067811865476)
    act = normed * below
    slope = below + normed * (jnp.exp(-0.5 * normed * normed) * 0.3989422804014327)
    return act, scaled, spread, slope


def norm_back(upstream, gain, scaled, spread, slope):
    inner = upstream * slope
    pushed = inner * gain
    back = spread * (
        pushed
        - jnp.mean(pushed, axis=-1, keepdims=True)
        - scaled * jnp.mean(pushed * scaled, axis=-1, keepdims=True)
    )
    return back, inner * scaled, inner


def fold_rows(array):
    return jnp.sum(array.reshape(array.shape[0] // 8, 8, array.shape[1]), axis=0)


def kernel(
    sizes,
    audio_hbm,
    send_hbm,
    place_hbm,
    cot_hbm,
    wz_hbm,
    w_hbm,
    gz_hbm,
    bz_hbm,
    g1_hbm,
    b1_hbm,
    feats_hbm,
    grad_ref,
    small_full,
    audio_ref,
    send_ref,
    place_ref,
    wz_ref,
    gz_ref,
    bz_ref,
    g1_ref,
    b1_ref,
    cot_ref,
    w_ref,
    feats_ref,
    msg,
    got_msg,
    arr,
    own_row,
    rim,
    samples,
    patches,
    wz_pad,
    act_even,
    act_odd,
    scaled_even,
    scaled_odd,
    slope_even,
    slope_odd,
    spread_even,
    spread_odd,
    third,
    back_one,
    back_f32,
    back_down,
    hi_even,
    lo_even,
    hi_odd,
    lo_odd,
    parts,
    got_core,
    sum_core,
    got_x,
    sum_x,
    got_y,
    got_y_first,
    sum_y_first,
    got_x_second,
    got_z,
    small,
    small_core,
    small_x,
    small_y,
    small_z,
    small_half,
    load_sems,
    near_send,
    near_recv,
    far_send,
    far_recv,
    rim_sems,
    core_send,
    core_recv,
    x_send,
    x_recv,
    y_send,
    y_recv,
    z_send,
    z_recv,
    sc_sems,
    sx_send,
    sx_recv,
    sy_send,
    sy_recv,
    sz_send,
    sz_recv,
    sf_sems,
    y_ready,
    z_ready,
):
    n_dp, n_x, n_z, n_rows, n_out, width = sizes
    n_even = n_out + tail_rows
    me = lax.axis_index("dp")
    z = lax.axis_index("seq")
    core = lax.rem(me, n_core)
    y = lax.rem(me // n_core, n_y)
    x = me // (n_core * n_y)

    def dp_of(px, py, pc):
        return (px * n_y + py) * n_core + pc

    n_near = n_x * n_core
    near = x * n_core + core

    def near_peer(k):
        at = lax.rem(near + k, n_near)
        return at, dp_of(at // n_core, y, lax.rem(at, n_core))

    def y_peer(k):
        at = lax.rem(y + k, n_y)
        return at, dp_of(x, at, core)

    barrier = pltpu.get_barrier_semaphore()

    def greet(axis, device):
        pl.semaphore_signal(barrier, inc=1, device_id={axis: device}, device_id_type=MESH)

    y_next = sorted({1, n_y - 1})
    z_next = sorted({1, n_z - 1})
    for k in z_next:
        greet("seq", lax.rem(z + k, n_z))
    for k in y_next:
        greet("dp", y_peer(k)[1])
    for k in range(1, n_near):
        greet("dp", near_peer(k)[1])

    def rounds(count, ready, axis, device):
        for _ in range(2, count // 2 + 1):
            for side, k in enumerate((1, count - 1)):
                pl.semaphore_signal(
                    ready.at[side], inc=1, device_id={axis: device(k)}, device_id_type=MESH
                )
            yield
            for side in range(2):
                pl.semaphore_wait(ready.at[side], 1)

    y_rounds = rounds(n_y, y_ready, "dp", lambda k: y_peer(k)[1])
    z_rounds = rounds(n_z, z_ready, "seq", lambda k: lax.rem(z + k, n_z))

    def step(some_rounds):
        next(some_rounds, None)

    def load(src, dst, at):
        copy = pltpu.make_async_copy(src, dst, load_sems.at[at])
        copy.start()
        return copy

    load_message = [load(audio_hbm, audio_ref, 3), load(send_hbm, send_ref, 4)]
    load_small = [
        load(src, dst, 5 + at)
        for at, (src, dst) in enumerate(
            (
                (place_hbm, place_ref),
                (wz_hbm, wz_ref),
                (gz_hbm, gz_ref),
                (bz_hbm, bz_ref),
                (g1_hbm, g1_ref),
                (b1_hbm, b1_ref),
            )
        )
    ]
    load_w = load(w_hbm, w_ref, 0)
    load_cot = load(cot_hbm, cot_ref, 1)

    spread_lanes = one_hot(
        jnp.bitwise_and(iota((40, lanes), 1), group - 1) == iota((40, lanes), 0)
    )
    for copy in load_message:
        copy.wait()
    blocks = dot(audio_ref[...], spread_lanes, TN).astype(BF16)
    chosen = one_hot(iota((n_rows, n_dp * slots), 0) == send_ref[...])
    picked = dot(chosen, blocks, TN)
    slot_of = jnp.bitwise_and(iota((n_dp * slots, lanes), 0), slots - 1)
    lane_group = lax.shift_right_logical(iota((n_dp * slots, lanes), 1), 6)
    in_group = slot_of == lane_group
    picked = jnp.where(in_group, picked, 0.0).astype(BF16)
    bit_y = n_y.bit_length() - 1

    def of_slot(shape, dim):
        device = lax.shift_right_logical(iota(shape, dim), 2)
        at_core = jnp.bitwise_and(device, n_core - 1)
        at_y = jnp.bitwise_and(lax.shift_right_logical(device, 1), n_y - 1)
        return lax.shift_right_logical(device, 1 + bit_y) * n_core + at_core, at_y

    slot_near, slot_y = of_slot((n_dp, n_dp * slots), 1)
    gather_dest = one_hot(slot_near * n_y + slot_y == iota((n_dp, n_dp * slots), 0))
    message = dot(gather_dest, picked)
    for d in range(n_dp):
        msg[d // n_y, d % n_y] = message[d : d + 1]

    pl.semaphore_wait(barrier, n_near - 1 + len(y_next) + len(z_next))
    step(y_rounds)
    step(z_rounds)

    def near_copy(k):
        at, device = near_peer(k)
        return pltpu.make_async_remote_copy(
            src_ref=msg.at[at],
            dst_ref=got_msg.at[near],
            send_sem=near_send.at[k],
            recv_sem=near_recv.at[k],
            device_id={"dp": device},
            device_id_type=MESH,
        )

    for k in range(1, n_near):
        near_copy(k).start()
    got_msg[near] = msg[near]

    for copy in load_small:
        copy.wait()
    wz_pad[...] = jnp.zeros_like(wz_pad)
    wz_pad[0:10, :] = wz_ref[...]
    gain_zero, bias_zero = gz_ref[...], bz_ref[...]
    gain_one, bias_one = g1_ref[...], b1_ref[...]
    keep = jnp.where(z < n_z - 1, 1.0, 0.0).astype(F32)
    placed = one_hot(iota((n_dp * slots, n_rows), 0) == place_ref[...])
    slot_near, slot_y = of_slot((n_dp * slots, n_dp), 0)
    spread_slots = one_hot(slot_y * n_near + slot_near == iota((n_dp * slots, n_dp), 1))
    step(y_rounds)
    lane_in, lane_out = iota((lanes, lanes), 0), iota((lanes, lanes), 1)
    sample_in = jnp.bitwise_and(lane_in, group - 1)
    sample_out = jnp.bitwise_and(lane_out, group - 1)
    fold_here = one_hot((sample_in == sample_out) & (sample_out < 40))
    fold_next = one_hot((sample_in + 40 == sample_out) & (sample_out < 45))
    row_id = iota((n_out, n_rows), 0)
    widen = one_hot(lax.shift_right_logical(row_id, 2) == iota((n_out, n_rows), 1))
    phase = jnp.bitwise_and(iota((n_out, lanes), 0), 3)
    own_phase = phase == lax.shift_right_logical(iota((n_out, lanes), 1), 6)
    step(y_rounds)
    tap = sample_in - 10 * lax.shift_right_logical(lane_in, 6)
    wanted = jnp.where(lane_out < 128, lane_out, lane_out - 128 + 5)
    limit = jnp.where(lane_out < 128, 10, 15)
    to_patch = one_hot((tap == wanted) & (wanted < limit))
    edge_from = jnp.where(lane_out < 128, lane_out, lane_out - 133)
    edge_limit = jnp.where(lane_out < 128, 10, 5)
    to_edge = one_hot((sample_in == edge_from) & (edge_from < edge_limit))

    for _ in range(n_y):
        step(y_rounds)
    for k in range(1, n_near):
        near_copy(k).wait_recv()

    def far_copy(k):
        at, device = y_peer(k)
        return pltpu.make_async_remote_copy(
            src_ref=got_msg.at[:, at],
            dst_ref=arr.at[y],
            send_sem=far_send.at[k],
            recv_sem=far_recv.at[k],
            device_id={"dp": device},
            device_id_type=MESH,
        )

    order_y = sorted(range(1, n_y), key=lambda k: -min(k, n_y - k))
    order_z = sorted(range(1, n_z), key=lambda k: -min(k, n_z - k))
    for k in order_y:
        far_copy(k).start()
    arr[y] = got_msg[:, y]
    for k in range(1, n_y):
        far_copy(k).wait_recv()

    received = jnp.concatenate(
        [arr[s // n_near, s % n_near] for s in range(n_dp)], axis=0
    ).astype(BF16)
    by_slot = dot(spread_slots, received)
    by_slot = jnp.where(in_group, by_slot, 0.0).astype(BF16)
    ordered = dot(placed, by_slot, TN)
    own_row[...] = dot(ordered[0:8].astype(BF16), to_edge)
    rim_copy = pltpu.make_async_remote_copy(
        src_ref=own_row,
        dst_ref=rim,
        send_sem=rim_sems.at[0],
        recv_sem=rim_sems.at[1],
        device_id={"seq": lax.rem(z + n_z - 1, n_z)},
        device_id_type=MESH,
    )
    rim_copy.start()
    samples[0:n_rows, :] = ordered
    samples[n_rows : n_rows + 8, :] = jnp.zeros((8, lanes), F32)
    wide = dot(samples[0:n_rows, :].astype(BF16), fold_here) + dot(
        samples[1 : n_rows + 1, :].astype(BF16), fold_next
    )
    rows = dot(widen, wide.astype(BF16))
    rows = jnp.where(own_phase, rows, 0.0).astype(BF16)
    patches[0:n_out, :] = dot(rows, to_patch).astype(BF16)

    step(z_rounds)
    def forward_even(r, n):
        pre = dot(patches[pl.ds(r, n), 0:128], wz_pad[...])
        act, scaled, spread, slope = norm_gelu(pre, gain_zero, bias_zero)
        scaled_even[pl.ds(r, n), :] = scaled
        slope_even[pl.ds(r, n), :] = slope
        spread_even[pl.ds(r, n), :] = spread
        return act

    def forward_odd(r, n):
        pre = dot(patches[pl.ds(r, n), 128:256], wz_pad[...])
        act, scaled, spread, slope = norm_gelu(pre, gain_zero, bias_zero)
        act_odd[pl.ds(r, n), :] = act.astype(BF16)
        scaled_odd[pl.ds(r, n), :] = scaled
        slope_odd[pl.ds(r, n), :] = slope
        spread_odd[pl.ds(r, n), :] = spread

    def forward_zero(i, carry):
        r = pl.multiple_of(i * chunk_zero, chunk_zero)
        act_even[pl.ds(r, chunk_zero), :] = forward_even(r, chunk_zero).astype(BF16)
        forward_odd(r, chunk_zero)
        return carry

    lax.fori_loop(0, n_out // chunk_zero, forward_zero, 0)

    step(z_rounds)
    rim_copy.wait_recv()
    edge = rim[0:1, :] * keep
    tail_id = iota((tail_rows, 128), 0)
    last = pl.ds(n_out - tail_rows, tail_rows)
    patches[last, 128:256] = (
        patches[last, 128:256].astype(F32)
        + jnp.where(tail_id == tail_rows - 1, edge[:, 128:256], 0.0)
    ).astype(BF16)
    patches[n_out:n_even, 0:128] = jnp.where(tail_id == 0, edge[:, 0:128], 0.0).astype(BF16)
    forward_odd(n_out - tail_rows, tail_rows)
    act_even[n_out:n_even, :] = (forward_even(n_out, tail_rows) * keep).astype(BF16)
    load_w.wait()

    step(z_rounds)
    third[...] = dot(act_even[...], w_ref[2 * width : 3 * width, :])
    for r in range(0, n_out, 64):
        third[r : r + 64, :] = third[r + 1 : r + 65, :]
    load_cot.wait()

    def layer_one(i, carry):
        sum_gain, sum_bias = carry
        r = pl.multiple_of(i * chunk_one, chunk_one)
        here = pl.ds(r, chunk_one)
        pre = (
            dot(act_even[here, :], w_ref[0:width, :])
            + dot(act_odd[here, :], w_ref[width : 2 * width, :])
            + third[here, :]
        )
        act, scaled, spread, slope = norm_gelu(pre, gain_one, bias_one)
        feats_ref[here, :] = act.astype(BF16)
        back, gain_term, bias_term = norm_back(
            cot_ref[here, :].astype(F32), gain_one, scaled, spread, slope
        )
        back = back.astype(BF16)
        back_one[here, :] = back
        back_f32[pl.ds(r + 8, chunk_one), :] = back.astype(F32)
        return (sum_gain + fold_rows(gain_term), sum_bias + fold_rows(bias_term))

    zero_sum = jnp.zeros((8, width), F32)
    back_f32[0:8, :] = jnp.zeros((8, width), F32)
    back_f32[n_out + 8 :, :] = jnp.zeros((back_f32.shape[0] - n_out - 8, width), F32)
    sum_gain_one, sum_bias_one = lax.fori_loop(
        0, n_out // chunk_one, layer_one, (zero_sum, zero_sum)
    )
    step(z_rounds)
    back_down[...] = back_f32[7 : 7 + n_even, :].astype(BF16)

    keep_feats = pltpu.make_async_copy(feats_ref, feats_hbm, load_sems.at[2])
    keep_feats.start()

    per_owner = 3 * width // 8 // n_dp
    cols = width // quarters
    partner = dp_of(x, y, 1 - core)

    def keep_pages(first_page, quarter, value):
        for i in range(width // 8):
            page = first_page + i
            d, j = page // per_owner, page % per_owner
            px, py, pc = d // (n_core * n_y), (d // n_core) % n_y, d % n_core
            for q in range(2):
                parts[quarter + q, pc, px, py, j] = value[
                    8 * i : 8 * i + 8, q * cols : (q + 1) * cols
                ].astype(BF16)

    def core_copy(q):
        return pltpu.make_async_remote_copy(
            src_ref=parts.at[q, 1 - core],
            dst_ref=got_core.at[q],
            send_sem=core_send.at[q],
            recv_sem=core_recv.at[q],
            device_id={"dp": partner},
            device_id_type=MESH,
        )

    for q in range(0, quarters, 2):
        here = slice(q * cols, (q + 2) * cols)
        keep_pages(0, q, dot(act_even[0:n_out, :], back_one[:, here], TN))
        keep_pages(width // 8, q, dot(act_odd[...], back_one[:, here], TN))
        keep_pages(2 * width // 8, q, dot(act_even[...], back_down[:, here], TN))
        core_copy(q).start()
        core_copy(q + 1).start()

    def back_zero(r, n, upstream, scaled_ref, slope_ref, spread_ref, hi_ref, lo_ref):
        here = pl.ds(r, n)
        back, gain_term, bias_term = norm_back(
            upstream, gain_zero, scaled_ref[here, :], spread_ref[here, :], slope_ref[here, :]
        )
        hi = back.astype(BF16)
        hi_ref[here, :] = hi
        lo_ref[here, :] = (back - hi.astype(F32)).astype(BF16)
        return fold_rows(gain_term), fold_rows(bias_term)

    def back_even(i, carry):
        r = pl.multiple_of(i * chunk_back, chunk_back)
        here = pl.ds(r, chunk_back)
        upstream = dot(back_one[here, :], w_ref[0:width, :], NT) + dot(
            back_down[here, :], w_ref[2 * width : 3 * width, :], NT
        )
        terms = back_zero(
            r, chunk_back, upstream, scaled_even, slope_even, spread_even, hi_even, lo_even
        )
        return (carry[0] + terms[0], carry[1] + terms[1])

    def back_odd(i, carry):
        r = pl.multiple_of(i * chunk_back, chunk_back)
        here = pl.ds(r, chunk_back)
        upstream = dot(back_one[here, :], w_ref[width : 2 * width, :], NT)
        terms = back_zero(
            r, chunk_back, upstream, scaled_odd, slope_odd, spread_odd, hi_odd, lo_odd
        )
        return (carry[0] + terms[0], carry[1] + terms[1])

    order_x = sorted(range(1, n_x), key=lambda k: -min(k, n_x - k))

    def x_peer(k):
        at = lax.rem(x + k, n_x)
        return at, dp_of(at, y, core)

    def send(src, dst, send_sem, recv_sem, axis, device):
        return pltpu.make_async_remote_copy(
            src_ref=src,
            dst_ref=dst,
            send_sem=send_sem,
            recv_sem=recv_sem,
            device_id={axis: device},
            device_id_type=MESH,
        )

    def x_copy(q, k):
        at, device = x_peer(k)
        src, dst = (
            (sum_y_first.at[at], got_x_second.at[k])
            if q == 0
            else (sum_core.at[q, at], got_x.at[q, k])
        )
        return send(src, dst, x_send.at[q, k], x_recv.at[q, k], "dp", device)

    def y_copy(q, k):
        at, device = y_peer(k)
        src, dst = (
            (sum_core.at[0, :, at], got_y_first.at[k])
            if q == 0
            else (sum_x.at[q, at], got_y.at[q, k])
        )
        return send(src, dst, y_send.at[q, k], y_recv.at[q, k], "dp", device)

    def pair_sum(q):
        core_copy(q).wait_recv()

        def add_core(i, carry):
            total = parts[q, core, i].astype(F32) + got_core[q, i].astype(F32)
            sum_core[q, i] = total.astype(BF16)
            return carry

        lax.fori_loop(0, n_x, add_core, 0)
        if q == 0:
            for k in order_y:
                y_copy(0, k).start()
        else:
            for k in order_x:
                x_copy(q, k).start()

    sums = back_even(0, (zero_sum, zero_sum))
    pair_sum(0)
    pair_sum(1)
    n_chunks = n_out // chunk_back
    if n_chunks > 1:
        sums = back_even(1, sums)
    pair_sum(2)
    pair_sum(3)
    for i in range(2, n_chunks):
        sums = back_even(i, sums)
    upstream = (
        dot(back_down[n_out:n_even, :], w_ref[2 * width : 3 * width, :], NT) * keep
    )
    terms = back_zero(
        n_out, tail_rows, upstream, scaled_even, slope_even, spread_even, hi_even, lo_even
    )
    sums = (sums[0] + terms[0], sums[1] + terms[1])
    sums = lax.fori_loop(0, n_chunks, back_odd, sums)

    grad_wz = (
        dot(patches[:, 0:128], hi_even[...], TN)
        + dot(patches[:, 0:128], lo_even[...], TN)
        + dot(patches[0:n_out, 128:256], hi_odd[...], TN)
        + dot(patches[0:n_out, 128:256], lo_odd[...], TN)
    )

    def row_sum(array):
        return jnp.sum(array, axis=0, keepdims=True)

    small[0, :, :] = grad_wz[0:8]
    small[1, 0:2, :] = grad_wz[8:10]
    small[1, 2:3, :] = row_sum(sums[0])
    small[1, 3:4, :] = row_sum(sums[1])
    small[1, 4:5, :] = row_sum(sum_gain_one)
    small[1, 5:6, :] = row_sum(sum_bias_one)
    small[1, 6:8, :] = jnp.zeros((2, width), F32)
    small_core_copy = pltpu.make_async_remote_copy(
        src_ref=small.at[1 - core],
        dst_ref=small_core,
        send_sem=sc_sems.at[0],
        recv_sem=sc_sems.at[1],
        device_id={"dp": partner},
        device_id_type=MESH,
    )
    small_core_copy.start()

    def share(buffer, at, sends, recvs, axis, device):
        def copy(k):
            return pltpu.make_async_remote_copy(
                src_ref=buffer.at[at],
                dst_ref=buffer.at[at],
                send_sem=sends.at[k],
                recv_sem=recvs.at[k],
                device_id={axis: device(k)},
                device_id_type=MESH,
            )

        return copy

    sx_copy = share(small_x, x, sx_send, sx_recv, "dp", lambda k: x_peer(k)[1])
    sy_copy = share(small_y, y, sy_send, sy_recv, "dp", lambda k: y_peer(k)[1])
    sz_copy = share(small_z, z, sz_send, sz_recv, "seq", lambda k: lax.rem(z + k, n_z))
    z_copies = [
        share(
            got_z.at[q], z, z_send.at[q], z_recv.at[q], "seq", lambda k: lax.rem(z + k, n_z)
        )
        for q in range(quarters)
    ]

    def total_of(buffer, count):
        total = buffer[0].astype(F32)
        for k in range(1, count):
            total = total + buffer[k].astype(F32)
        return total

    def plus_got(total, buffer, count):
        total = total.astype(F32)
        for k in range(1, count):
            total = total + buffer[k].astype(F32)
        return total.astype(BF16)

    def got_all(copy, count):
        for k in range(1, count):
            copy(k).wait_recv()

    def along_y(q):
        got_all(functools.partial(x_copy, q), n_x)
        sum_x[q] = plus_got(sum_core[q, x], got_x.at[q], n_x)
        for k in order_y:
            y_copy(q, k).start()

    def along_z(q):
        if q == 0:
            got_all(functools.partial(x_copy, 0), n_x)
            got_z[0, z] = plus_got(sum_y_first[x], got_x_second, n_x)
        else:
            got_all(functools.partial(y_copy, q), n_y)
            got_z[q, z] = plus_got(sum_x[q, y], got_y.at[q], n_y)
        for k in order_z:
            z_copies[q](k).start()

    def finish(q):
        got_all(z_copies[q], n_z)
        total = total_of(got_z.at[q], n_z)
        for j in range(per_owner):
            grad_ref[8 * j : 8 * j + 8, q * cols : (q + 1) * cols] = total[j]

    for _ in range(n_z):
        step(z_rounds)
    along_y(1)
    small_core_copy.wait_recv()
    small_z[z] = (small[core] + small_core[...]).astype(BF16)
    for k in order_z:
        sz_copy(k).start()
    along_y(2)
    got_all(functools.partial(y_copy, 0), n_y)
    sum_y_first[...] = plus_got(sum_core[0, :, y], got_y_first, n_y)
    for k in order_x:
        x_copy(0, k).start()
    along_y(3)
    along_z(1)
    along_z(0)
    got_all(sz_copy, n_z)
    small_x[x] = total_of(small_z, n_z)
    for k in order_x:
        sx_copy(k).start()
    along_z(2)
    got_all(sx_copy, n_x)
    small_y[y] = total_of(small_x, n_x)
    for k in order_y:
        sy_copy(k).start()
    along_z(3)
    finish(1)
    finish(0)
    got_all(sy_copy, n_y)
    total = total_of(small_y, n_y)
    small_half[...] = total
    full_copy = send(
        small_half, small_full.at[core], sf_sems.at[0], sf_sems.at[1], "dp", partner
    )
    full_copy.start()
    small_full[core] = total
    finish(2)
    finish(3)
    full_copy.wait_recv()

    keep_feats.wait()
    rim_copy.wait_send()
    small_core_copy.wait_send()
    full_copy.wait_send()
    for k in range(1, n_near):
        near_copy(k).wait_send()
    for k in range(1, n_x):
        sx_copy(k).wait_send()
    for k in range(1, n_y):
        far_copy(k).wait_send()
        sy_copy(k).wait_send()
    for k in range(1, n_z):
        sz_copy(k).wait_send()
    for q in range(quarters):
        core_copy(q).wait_send()
        for k in range(1, n_x):
            x_copy(q, k).wait_send()
        for k in range(1, n_y):
            y_copy(q, k).wait_send()
        for k in range(1, n_z):
            z_copies[q](k).wait_send()


def hand_out(
    feats_in, grad_in, small_ref, feats_ref, grad_ref, gwz_ref, ggz_ref, gbz_ref, gg1_ref, gb1_ref
):
    feats_ref[...] = feats_in[...]
    grad_ref[...] = grad_in[...]
    gwz_ref[0:8, :] = small_ref[0]
    rest = small_ref[1]
    gwz_ref[8:10, :] = rest[0:2]
    ggz_ref[...] = rest[2:3]
    gbz_ref[...] = rest[3:4]
    gg1_ref[...] = rest[4:5]
    gb1_ref[...] = rest[5:6]


def on_device(n_dp, n_z, audio, send, place, cot, conv_zero, conv_one, gz, bz, g1, b1):
    n_x = n_dp // (n_core * n_y)
    n_rows, n_out, width = audio.shape[1], cot.shape[1], cot.shape[2]
    n_even = n_out + tail_rows
    per_owner = 3 * width // 8 // n_dp
    n_near = n_x * n_core
    vmem = lambda *shape, dtype=F32: pltpu.VMEM(shape, dtype)
    page = lambda *shape: pltpu.VMEM((*shape, per_owner, 8, width // quarters), BF16)
    dma = lambda *shape: pltpu.SemaphoreType.DMA(shape)
    scratch = [
        vmem(40, n_rows, dtype=BF16),
        vmem(1, n_dp * slots, dtype=jnp.int32),
        vmem(1, n_rows, dtype=jnp.int32),
        vmem(10, width, dtype=BF16),
        *[vmem(1, width)] * 4,
        vmem(n_out, width, dtype=BF16),
        vmem(3 * width, width, dtype=BF16),
        vmem(n_out, width, dtype=BF16),
        vmem(n_near, n_y, 1, lanes),
        vmem(n_near, n_y, 1, lanes),
        vmem(n_y, n_near, 1, lanes),
        vmem(8, lanes),
        vmem(8, lanes),
        vmem(n_rows + 8, lanes),
        vmem(n_even, lanes, dtype=BF16),
        vmem(128, width, dtype=BF16),
        vmem(n_even, width, dtype=BF16),
        vmem(n_out, width, dtype=BF16),
        vmem(n_even, width),
        vmem(n_out, width),
        vmem(n_even, width),
        vmem(n_out, width),
        vmem(n_even, 1),
        vmem(n_out, 1),
        vmem(n_even, width),
        vmem(n_out, width, dtype=BF16),
        vmem(n_out + 32, width),
        vmem(n_even, width, dtype=BF16),
        vmem(n_even, width, dtype=BF16),
        vmem(n_even, width, dtype=BF16),
        vmem(n_out, width, dtype=BF16),
        vmem(n_out, width, dtype=BF16),
        page(quarters, n_core, n_x, n_y),
        page(quarters, n_x, n_y),
        page(quarters, n_x, n_y),
        page(quarters, n_x, n_y),
        page(quarters, n_y),
        page(quarters, n_y),
        page(n_y, n_x),
        page(n_x),
        page(n_x),
        page(quarters, n_z),
        vmem(2, 8, width),
        vmem(8, width),
        vmem(n_x, 8, width),
        vmem(n_y, 8, width),
        vmem(n_z, 8, width, dtype=BF16),
        vmem(8, width),
        dma(11),
        dma(n_near),
        dma(n_near),
        dma(n_y),
        dma(n_y),
        dma(2),
        dma(quarters),
        dma(quarters),
        dma(quarters, n_x),
        dma(quarters, n_x),
        dma(quarters, n_y),
        dma(quarters, n_y),
        dma(quarters, n_z),
        dma(quarters, n_z),
        dma(2),
        dma(n_x),
        dma(n_x),
        dma(n_y),
        dma(n_y),
        dma(n_z),
        dma(n_z),
        dma(2),
        pltpu.SemaphoreType.REGULAR((2,)),
        pltpu.SemaphoreType.REGULAR((2,)),
    ]
    row = jax.ShapeDtypeStruct((1, width), F32)
    in_vmem = pl.BlockSpec(memory_space=pltpu.VMEM)
    anywhere = pl.BlockSpec(memory_space=pl.ANY)
    feats, grad, small = pl.pallas_call(
        functools.partial(kernel, (n_dp, n_x, n_z, n_rows, n_out, width)),
        out_shape=(
            jax.ShapeDtypeStruct((n_out, width), BF16),
            jax.ShapeDtypeStruct((3 * width // n_dp, width), F32),
            jax.ShapeDtypeStruct((2, 8, width), F32),
        ),
        in_specs=[anywhere] * 10,
        out_specs=(anywhere, in_vmem, in_vmem),
        scratch_shapes=scratch,
        compiler_params=pltpu.CompilerParams(
            collective_id=0, has_side_effects=True, vmem_limit_bytes=60 * 2**20
        ),
    )(
        audio[0].T,
        send.reshape(1, -1),
        place.reshape(1, -1),
        cot[0],
        conv_zero,
        conv_one,
        gz[None],
        bz[None],
        g1[None],
        b1[None],
    )
    feats, grad, gwz, ggz, gbz, gg1, gb1 = pl.pallas_call(
        hand_out,
        out_shape=(
            jax.ShapeDtypeStruct(feats.shape, feats.dtype),
            jax.ShapeDtypeStruct(grad.shape, grad.dtype),
            jax.ShapeDtypeStruct((10, width), F32),
            row,
            row,
            row,
            row,
        ),
        in_specs=[in_vmem] * 3,
        out_specs=(in_vmem,) * 7,
        compiler_params=pltpu.CompilerParams(vmem_limit_bytes=60 * 2**20),
    )(feats, grad, small)
    return feats[None], grad, gwz, ggz[0], gbz[0], gg1[0], gb1[0]


def solution(mesh):
    placed = (
        P("dp", "seq", None),
        P("seq", "dp", None),
        P("seq", "dp", None),
        P("dp", "seq", None),
        P(),
        P(),
        P(),
        P(),
        P(),
        P(),
    )
    return jax.shard_map(
        functools.partial(on_device, mesh.shape["dp"], mesh.shape["seq"]),
        mesh=mesh,
        in_specs=placed,
        out_specs=(P("dp", "seq", None), P("dp", None), P(), P(), P(), P(), P()),
        check_vma=False,
    )
```

```python
import functools

import jax
import jax.numpy as jnp
from jax import lax
from jax.experimental import pallas as pl
from jax.experimental.pallas import tpu as pltpu
from jax.sharding import PartitionSpec as P

MESH = pl.DeviceIdType.MESH
F32 = jnp.float32
BF16 = jnp.bfloat16
norm_eps = 1e-05
n_core = 2
n_y = 8
slots = 4
group = 64
lanes = slots * group
chunk_zero = 512
chunk_one = 512
chunk_back = 256
tail_rows = 16
quarters = 4


def iota(shape, dim):
    return lax.broadcasted_iota(jnp.int32, shape, dim)


def one_hot(mask):
    return jnp.where(mask, 1.0, 0.0).astype(BF16)


def dot(a, b, dims=((1,), (0,))):
    return lax.dot_general(a, b, (dims, ((), ())), preferred_element_type=F32)


TN = ((0,), (0,))
NT = ((1,), (1,))


def norm_gelu(pre, gain, bias):
    center = pre - jnp.mean(pre, axis=-1, keepdims=True)
    spread = lax.rsqrt(jnp.mean(center * center, axis=-1, keepdims=True) + norm_eps)
    scaled = center * spread
    normed = scaled * gain + bias
    below = 0.5 + 0.5 * lax.erf(normed * 0.7071067811865476)
    act = normed * below
    slope = below + normed * (jnp.exp(-0.5 * normed * normed) * 0.3989422804014327)
    return act, scaled, spread, slope


def norm_back(upstream, gain, scaled, spread, slope):
    inner = upstream * slope
    pushed = inner * gain
    back = spread * (
        pushed
        - jnp.mean(pushed, axis=-1, keepdims=True)
        - scaled * jnp.mean(pushed * scaled, axis=-1, keepdims=True)
    )
    return back, inner * scaled, inner


def fold_rows(array):
    return jnp.sum(array.reshape(array.shape[0] // 8, 8, array.shape[1]), axis=0)


def kernel(
    sizes,
    audio_hbm,
    send_hbm,
    place_hbm,
    cot_hbm,
    wz_hbm,
    w_hbm,
    gz_hbm,
    bz_hbm,
    g1_hbm,
    b1_hbm,
    feats_hbm,
    grad_ref,
    small_full,
    audio_ref,
    send_ref,
    place_ref,
    wz_ref,
    gz_ref,
    bz_ref,
    g1_ref,
    b1_ref,
    cot_ref,
    w_ref,
    feats_ref,
    msg,
    got_msg,
    arr,
    own_row,
    rim,
    samples,
    patches,
    wz_pad,
    act_even,
    act_odd,
    scaled_even,
    scaled_odd,
    slope_even,
    slope_odd,
    spread_even,
    spread_odd,
    third,
    back_one,
    back_f32,
    back_down,
    hi_even,
    lo_even,
    hi_odd,
    lo_odd,
    parts,
    got_core,
    sum_core,
    got_x,
    sum_x,
    got_y,
    got_y_first,
    sum_y_first,
    got_x_second,
    got_z,
    small,
    small_core,
    small_x,
    small_y,
    small_z,
    small_half,
    load_sems,
    near_send,
    near_recv,
    far_send,
    far_recv,
    rim_sems,
    core_send,
    core_recv,
    x_send,
    x_recv,
    y_send,
    y_recv,
    z_send,
    z_recv,
    sc_sems,
    sx_send,
    sx_recv,
    sy_send,
    sy_recv,
    sz_send,
    sz_recv,
    sf_sems,
    y_ready,
    z_ready,
):
    n_dp, n_x, n_z, n_rows, n_out, width = sizes
    n_even = n_out + tail_rows
    me = lax.axis_index("dp")
    z = lax.axis_index("seq")
    core = lax.rem(me, n_core)
    y = lax.rem(me // n_core, n_y)
    x = me // (n_core * n_y)

    def dp_of(px, py, pc):
        return (px * n_y + py) * n_core + pc

    n_near = n_x * n_core
    near = x * n_core + core

    def near_peer(k):
        at = lax.rem(near + k, n_near)
        return at, dp_of(at // n_core, y, lax.rem(at, n_core))

    def y_peer(k):
        at = lax.rem(y + k, n_y)
        return at, dp_of(x, at, core)

    barrier = pltpu.get_barrier_semaphore()

    def greet(axis, device):
        pl.semaphore_signal(barrier, inc=1, device_id={axis: device}, device_id_type=MESH)

    y_next = sorted({1, n_y - 1})
    z_next = sorted({1, n_z - 1})
    for k in z_next:
        greet("seq", lax.rem(z + k, n_z))
    for k in y_next:
        greet("dp", y_peer(k)[1])
    for k in range(1, n_near):
        greet("dp", near_peer(k)[1])

    def rounds(count, ready, axis, device):
        for _ in range(2, count // 2 + 1):
            for side, k in enumerate((1, count - 1)):
                pl.semaphore_signal(
                    ready.at[side], inc=1, device_id={axis: device(k)}, device_id_type=MESH
                )
            yield
            for side in range(2):
                pl.semaphore_wait(ready.at[side], 1)

    y_rounds = rounds(n_y, y_ready, "dp", lambda k: y_peer(k)[1])
    z_rounds = rounds(n_z, z_ready, "seq", lambda k: lax.rem(z + k, n_z))

    def step(some_rounds):
        next(some_rounds, None)

    def load(src, dst, at):
        copy = pltpu.make_async_copy(src, dst, load_sems.at[at])
        copy.start()
        return copy

    load_message = [load(audio_hbm, audio_ref, 3), load(send_hbm, send_ref, 4)]
    load_small = [
        load(src, dst, 5 + at)
        for at, (src, dst) in enumerate(
            (
                (place_hbm, place_ref),
                (wz_hbm, wz_ref),
                (gz_hbm, gz_ref),
                (bz_hbm, bz_ref),
                (g1_hbm, g1_ref),
                (b1_hbm, b1_ref),
            )
        )
    ]
    load_w = load(w_hbm, w_ref, 0)
    load_cot = load(cot_hbm, cot_ref, 1)

    spread_lanes = one_hot(
        jnp.bitwise_and(iota((40, lanes), 1), group - 1) == iota((40, lanes), 0)
    )
    for copy in load_message:
        copy.wait()
    blocks = dot(audio_ref[...], spread_lanes, TN).astype(BF16)
    chosen = one_hot(iota((n_rows, n_dp * slots), 0) == send_ref[...])
    picked = dot(chosen, blocks, TN)
    slot_of = jnp.bitwise_and(iota((n_dp * slots, lanes), 0), slots - 1)
    lane_group = lax.shift_right_logical(iota((n_dp * slots, lanes), 1), 6)
    in_group = slot_of == lane_group
    picked = jnp.where(in_group, picked, 0.0).astype(BF16)
    bit_y = n_y.bit_length() - 1

    def of_slot(shape, dim):
        device = lax.shift_right_logical(iota(shape, dim), 2)
        at_core = jnp.bitwise_and(device, n_core - 1)
        at_y = jnp.bitwise_and(lax.shift_right_logical(device, 1), n_y - 1)
        return lax.shift_right_logical(device, 1 + bit_y) * n_core + at_core, at_y

    slot_near, slot_y = of_slot((n_dp, n_dp * slots), 1)
    gather_dest = one_hot(slot_near * n_y + slot_y == iota((n_dp, n_dp * slots), 0))
    message = dot(gather_dest, picked)
    for d in range(n_dp):
        msg[d // n_y, d % n_y] = message[d : d + 1]

    pl.semaphore_wait(barrier, n_near - 1 + len(y_next) + len(z_next))
    step(y_rounds)
    step(z_rounds)

    def near_copy(k):
        at, device = near_peer(k)
        return pltpu.make_async_remote_copy(
            src_ref=msg.at[at],
            dst_ref=got_msg.at[near],
            send_sem=near_send.at[k],
            recv_sem=near_recv.at[k],
            device_id={"dp": device},
            device_id_type=MESH,
        )

    for k in range(1, n_near):
        near_copy(k).start()
    got_msg[near] = msg[near]

    for copy in load_small:
        copy.wait()
    wz_pad[...] = jnp.zeros_like(wz_pad)
    wz_pad[0:10, :] = wz_ref[...]
    gain_zero, bias_zero = gz_ref[...], bz_ref[...]
    gain_one, bias_one = g1_ref[...], b1_ref[...]
    keep = jnp.where(z < n_z - 1, 1.0, 0.0).astype(F32)
    placed = one_hot(iota((n_dp * slots, n_rows), 0) == place_ref[...])
    slot_near, slot_y = of_slot((n_dp * slots, n_dp), 0)
    spread_slots = one_hot(slot_y * n_near + slot_near == iota((n_dp * slots, n_dp), 1))
    step(y_rounds)
    lane_in, lane_out = iota((lanes, lanes), 0), iota((lanes, lanes), 1)
    sample_in = jnp.bitwise_and(lane_in, group - 1)
    sample_out = jnp.bitwise_and(lane_out, group - 1)
    fold_here = one_hot((sample_in == sample_out) & (sample_out < 40))
    fold_next = one_hot((sample_in + 40 == sample_out) & (sample_out < 45))
    row_id = iota((n_out, n_rows), 0)
    widen = one_hot(lax.shift_right_logical(row_id, 2) == iota((n_out, n_rows), 1))
    phase = jnp.bitwise_and(iota((n_out, lanes), 0), 3)
    own_phase = phase == lax.shift_right_logical(iota((n_out, lanes), 1), 6)
    step(y_rounds)
    tap = sample_in - 10 * lax.shift_right_logical(lane_in, 6)
    wanted = jnp.where(lane_out < 128, lane_out, lane_out - 128 + 5)
    limit = jnp.where(lane_out < 128, 10, 15)
    to_patch = one_hot((tap == wanted) & (wanted < limit))
    edge_from = jnp.where(lane_out < 128, lane_out, lane_out - 133)
    edge_limit = jnp.where(lane_out < 128, 10, 5)
    to_edge = one_hot((sample_in == edge_from) & (edge_from < edge_limit))

    for _ in range(n_y):
        step(y_rounds)
    for k in range(1, n_near):
        near_copy(k).wait_recv()

    def far_copy(k):
        at, device = y_peer(k)
        return pltpu.make_async_remote_copy(
            src_ref=got_msg.at[:, at],
            dst_ref=arr.at[y],
            send_sem=far_send.at[k],
            recv_sem=far_recv.at[k],
            device_id={"dp": device},
            device_id_type=MESH,
        )

    order_y = sorted(range(1, n_y), key=lambda k: -min(k, n_y - k))
    order_z = sorted(range(1, n_z), key=lambda k: -min(k, n_z - k))
    for k in order_y:
        far_copy(k).start()
    arr[y] = got_msg[:, y]
    for k in range(1, n_y):
        far_copy(k).wait_recv()

    received = jnp.concatenate(
        [arr[s // n_near, s % n_near] for s in range(n_dp)], axis=0
    ).astype(BF16)
    by_slot = dot(spread_slots, received)
    by_slot = jnp.where(in_group, by_slot, 0.0).astype(BF16)
    ordered = dot(placed, by_slot, TN)
    own_row[...] = dot(ordered[0:8].astype(BF16), to_edge)
    rim_copy = pltpu.make_async_remote_copy(
        src_ref=own_row,
        dst_ref=rim,
        send_sem=rim_sems.at[0],
        recv_sem=rim_sems.at[1],
        device_id={"seq": lax.rem(z + n_z - 1, n_z)},
        device_id_type=MESH,
    )
    rim_copy.start()
    samples[0:n_rows, :] = ordered
    samples[n_rows : n_rows + 8, :] = jnp.zeros((8, lanes), F32)
    wide = dot(samples[0:n_rows, :].astype(BF16), fold_here) + dot(
        samples[1 : n_rows + 1, :].astype(BF16), fold_next
    )
    rows = dot(widen, wide.astype(BF16))
    rows = jnp.where(own_phase, rows, 0.0).astype(BF16)
    patches[0:n_out, :] = dot(rows, to_patch).astype(BF16)

    step(z_rounds)
    def forward_even(r, n):
        pre = dot(patches[pl.ds(r, n), 0:128], wz_pad[...])
        act, scaled, spread, slope = norm_gelu(pre, gain_zero, bias_zero)
        scaled_even[pl.ds(r, n), :] = scaled
        slope_even[pl.ds(r, n), :] = slope
        spread_even[pl.ds(r, n), :] = spread
        return act

    def forward_odd(r, n):
        pre = dot(patches[pl.ds(r, n), 128:256], wz_pad[...])
        act, scaled, spread, slope = norm_gelu(pre, gain_zero, bias_zero)
        act_odd[pl.ds(r, n), :] = act.astype(BF16)
        scaled_odd[pl.ds(r, n), :] = scaled
        slope_odd[pl.ds(r, n), :] = slope
        spread_odd[pl.ds(r, n), :] = spread

    def forward_zero(i, carry):
        r = pl.multiple_of(i * chunk_zero, chunk_zero)
        act_even[pl.ds(r, chunk_zero), :] = forward_even(r, chunk_zero).astype(BF16)
        forward_odd(r, chunk_zero)
        return carry

    lax.fori_loop(0, n_out // chunk_zero, forward_zero, 0)

    step(z_rounds)
    rim_copy.wait_recv()
    edge = rim[0:1, :] * keep
    tail_id = iota((tail_rows, 128), 0)
    last = pl.ds(n_out - tail_rows, tail_rows)
    patches[last, 128:256] = (
        patches[last, 128:256].astype(F32)
        + jnp.where(tail_id == tail_rows - 1, edge[:, 128:256], 0.0)
    ).astype(BF16)
    patches[n_out:n_even, 0:128] = jnp.where(tail_id == 0, edge[:, 0:128], 0.0).astype(BF16)
    forward_odd(n_out - tail_rows, tail_rows)
    act_even[n_out:n_even, :] = (forward_even(n_out, tail_rows) * keep).astype(BF16)
    load_w.wait()

    step(z_rounds)
    third[...] = dot(act_even[...], w_ref[2 * width : 3 * width, :])
    for r in range(0, n_out, 64):
        third[r : r + 64, :] = third[r + 1 : r + 65, :]
    load_cot.wait()

    def layer_one(i, carry):
        sum_gain, sum_bias = carry
        r = pl.multiple_of(i * chunk_one, chunk_one)
        here = pl.ds(r, chunk_one)
        pre = (
            dot(act_even[here, :], w_ref[0:width, :])
            + dot(act_odd[here, :], w_ref[width : 2 * width, :])
            + third[here, :]
        )
        act, scaled, spread, slope = norm_gelu(pre, gain_one, bias_one)
        feats_ref[here, :] = act.astype(BF16)
        back, gain_term, bias_term = norm_back(
            cot_ref[here, :].astype(F32), gain_one, scaled, spread, slope
        )
        back = back.astype(BF16)
        back_one[here, :] = back
        back_f32[pl.ds(r + 8, chunk_one), :] = back.astype(F32)
        return (sum_gain + fold_rows(gain_term), sum_bias + fold_rows(bias_term))

    zero_sum = jnp.zeros((8, width), F32)
    back_f32[0:8, :] = jnp.zeros((8, width), F32)
    back_f32[n_out + 8 :, :] = jnp.zeros((back_f32.shape[0] - n_out - 8, width), F32)
    sum_gain_one, sum_bias_one = lax.fori_loop(
        0, n_out // chunk_one, layer_one, (zero_sum, zero_sum)
    )
    step(z_rounds)
    back_down[...] = back_f32[7 : 7 + n_even, :].astype(BF16)

    keep_feats = pltpu.make_async_copy(feats_ref, feats_hbm, load_sems.at[2])
    keep_feats.start()

    per_owner = 3 * width // 8 // n_dp
    cols = width // quarters
    partner = dp_of(x, y, 1 - core)

    def keep_pages(first_page, quarter, value):
        for i in range(width // 8):
            page = first_page + i
            d, j = page // per_owner, page % per_owner
            px, py, pc = d // (n_core * n_y), (d // n_core) % n_y, d % n_core
            for q in range(2):
                parts[quarter + q, pc, px, py, j] = value[
                    8 * i : 8 * i + 8, q * cols : (q + 1) * cols
                ].astype(BF16)

    def core_copy(q):
        return pltpu.make_async_remote_copy(
            src_ref=parts.at[q, 1 - core],
            dst_ref=got_core.at[q],
            send_sem=core_send.at[q],
            recv_sem=core_recv.at[q],
            device_id={"dp": partner},
            device_id_type=MESH,
        )

    for q in range(0, quarters, 2):
        here = slice(q * cols, (q + 2) * cols)
        keep_pages(0, q, dot(act_even[0:n_out, :], back_one[:, here], TN))
        keep_pages(width // 8, q, dot(act_odd[...], back_one[:, here], TN))
        keep_pages(2 * width // 8, q, dot(act_even[...], back_down[:, here], TN))
        core_copy(q).start()
        core_copy(q + 1).start()

    def back_zero(r, n, upstream, scaled_ref, slope_ref, spread_ref, hi_ref, lo_ref):
        here = pl.ds(r, n)
        back, gain_term, bias_term = norm_back(
            upstream, gain_zero, scaled_ref[here, :], spread_ref[here, :], slope_ref[here, :]
        )
        hi = back.astype(BF16)
        hi_ref[here, :] = hi
        lo_ref[here, :] = (back - hi.astype(F32)).astype(BF16)
        return fold_rows(gain_term), fold_rows(bias_term)

    def back_even(i, carry):
        r = pl.multiple_of(i * chunk_back, chunk_back)
        here = pl.ds(r, chunk_back)
        upstream = dot(back_one[here, :], w_ref[0:width, :], NT) + dot(
            back_down[here, :], w_ref[2 * width : 3 * width, :], NT
        )
        terms = back_zero(
            r, chunk_back, upstream, scaled_even, slope_even, spread_even, hi_even, lo_even
        )
        return (carry[0] + terms[0], carry[1] + terms[1])

    def back_odd(i, carry):
        r = pl.multiple_of(i * chunk_back, chunk_back)
        here = pl.ds(r, chunk_back)
        upstream = dot(back_one[here, :], w_ref[width : 2 * width, :], NT)
        terms = back_zero(
            r, chunk_back, upstream, scaled_odd, slope_odd, spread_odd, hi_odd, lo_odd
        )
        return (carry[0] + terms[0], carry[1] + terms[1])

    order_x = sorted(range(1, n_x), key=lambda k: -min(k, n_x - k))

    def x_peer(k):
        at = lax.rem(x + k, n_x)
        return at, dp_of(at, y, core)

    def send(src, dst, send_sem, recv_sem, axis, device):
        return pltpu.make_async_remote_copy(
            src_ref=src,
            dst_ref=dst,
            send_sem=send_sem,
            recv_sem=recv_sem,
            device_id={axis: device},
            device_id_type=MESH,
        )

    def x_copy(q, k):
        at, device = x_peer(k)
        src, dst = (
            (sum_y_first.at[at], got_x_second.at[k])
            if q == 0
            else (sum_core.at[q, at], got_x.at[q, k])
        )
        return send(src, dst, x_send.at[q, k], x_recv.at[q, k], "dp", device)

    def y_copy(q, k):
        at, device = y_peer(k)
        src, dst = (
            (sum_core.at[0, :, at], got_y_first.at[k])
            if q == 0
            else (sum_x.at[q, at], got_y.at[q, k])
        )
        return send(src, dst, y_send.at[q, k], y_recv.at[q, k], "dp", device)

    def pair_sum(q):
        core_copy(q).wait_recv()

        def add_core(i, carry):
            total = parts[q, core, i].astype(F32) + got_core[q, i].astype(F32)
            sum_core[q, i] = total.astype(BF16)
            return carry

        lax.fori_loop(0, n_x, add_core, 0)
        if q == 0:
            for k in order_y:
                y_copy(0, k).start()
        else:
            for k in order_x:
                x_copy(q, k).start()

    sums = back_even(0, (zero_sum, zero_sum))
    pair_sum(0)
    pair_sum(1)
    n_chunks = n_out // chunk_back
    if n_chunks > 1:
        sums = back_even(1, sums)
    pair_sum(2)
    pair_sum(3)
    for i in range(2, n_chunks):
        sums = back_even(i, sums)
    upstream = (
        dot(back_down[n_out:n_even, :], w_ref[2 * width : 3 * width, :], NT) * keep
    )
    terms = back_zero(
        n_out, tail_rows, upstream, scaled_even, slope_even, spread_even, hi_even, lo_even
    )
    sums = (sums[0] + terms[0], sums[1] + terms[1])
    sums = lax.fori_loop(0, n_chunks, back_odd, sums)

    grad_wz = (
        dot(patches[:, 0:128], hi_even[...], TN)
        + dot(patches[:, 0:128], lo_even[...], TN)
        + dot(patches[0:n_out, 128:256], hi_odd[...], TN)
        + dot(patches[0:n_out, 128:256], lo_odd[...], TN)
    )

    def row_sum(array):
        return jnp.sum(array, axis=0, keepdims=True)

    small[0, :, :] = grad_wz[0:8]
    small[1, 0:2, :] = grad_wz[8:10]
    small[1, 2:3, :] = row_sum(sums[0])
    small[1, 3:4, :] = row_sum(sums[1])
    small[1, 4:5, :] = row_sum(sum_gain_one)
    small[1, 5:6, :] = row_sum(sum_bias_one)
    small[1, 6:8, :] = jnp.zeros((2, width), F32)
    small_core_copy = pltpu.make_async_remote_copy(
        src_ref=small.at[1 - core],
        dst_ref=small_core,
        send_sem=sc_sems.at[0],
        recv_sem=sc_sems.at[1],
        device_id={"dp": partner},
        device_id_type=MESH,
    )
    small_core_copy.start()

    def share(buffer, at, sends, recvs, axis, device):
        def copy(k):
            return pltpu.make_async_remote_copy(
                src_ref=buffer.at[at],
                dst_ref=buffer.at[at],
                send_sem=sends.at[k],
                recv_sem=recvs.at[k],
                device_id={axis: device(k)},
                device_id_type=MESH,
            )

        return copy

    sx_copy = share(small_x, x, sx_send, sx_recv, "dp", lambda k: x_peer(k)[1])
    sy_copy = share(small_y, y, sy_send, sy_recv, "dp", lambda k: y_peer(k)[1])
    sz_copy = share(small_z, z, sz_send, sz_recv, "seq", lambda k: lax.rem(z + k, n_z))
    z_copies = [
        share(
            got_z.at[q], z, z_send.at[q], z_recv.at[q], "seq", lambda k: lax.rem(z + k, n_z)
        )
        for q in range(quarters)
    ]

    def total_of(buffer, count):
        total = buffer[0].astype(F32)
        for k in range(1, count):
            total = total + buffer[k].astype(F32)
        return total

    def plus_got(total, buffer, count):
        total = total.astype(F32)
        for k in range(1, count):
            total = total + buffer[k].astype(F32)
        return total.astype(BF16)

    def got_all(copy, count):
        for k in range(1, count):
            copy(k).wait_recv()

    def along_y(q):
        got_all(functools.partial(x_copy, q), n_x)
        sum_x[q] = plus_got(sum_core[q, x], got_x.at[q], n_x)
        for k in order_y:
            y_copy(q, k).start()

    def along_z(q):
        if q == 0:
            got_all(functools.partial(x_copy, 0), n_x)
            got_z[0, z] = plus_got(sum_y_first[x], got_x_second, n_x)
        else:
            got_all(functools.partial(y_copy, q), n_y)
            got_z[q, z] = plus_got(sum_x[q, y], got_y.at[q], n_y)
        for k in order_z:
            z_copies[q](k).start()

    def finish(q):
        got_all(z_copies[q], n_z)
        total = total_of(got_z.at[q], n_z)
        for j in range(per_owner):
            grad_ref[8 * j : 8 * j + 8, q * cols : (q + 1) * cols] = total[j]

    for _ in range(n_z):
        step(z_rounds)
    along_y(1)
    small_core_copy.wait_recv()
    small_z[z] = (small[core] + small_core[...]).astype(BF16)
    for k in order_z:
        sz_copy(k).start()
    along_y(2)
    got_all(functools.partial(y_copy, 0), n_y)
    sum_y_first[...] = plus_got(sum_core[0, :, y], got_y_first, n_y)
    for k in order_x:
        x_copy(0, k).start()
    along_y(3)
    along_z(1)
    along_z(0)
    got_all(sz_copy, n_z)
    small_x[x] = total_of(small_z, n_z)
    for k in order_x:
        sx_copy(k).start()
    along_z(2)
    got_all(sx_copy, n_x)
    small_y[y] = total_of(small_x, n_x)
    for k in order_y:
        sy_copy(k).start()
    along_z(3)
    finish(1)
    finish(0)
    got_all(sy_copy, n_y)
    total = total_of(small_y, n_y)
    small_half[...] = total
    full_copy = send(
        small_half, small_full.at[core], sf_sems.at[0], sf_sems.at[1], "dp", partner
    )
    full_copy.start()
    small_full[core] = total
    finish(2)
    finish(3)
    full_copy.wait_recv()

    keep_feats.wait()
    rim_copy.wait_send()
    small_core_copy.wait_send()
    full_copy.wait_send()
    for k in range(1, n_near):
        near_copy(k).wait_send()
    for k in range(1, n_x):
        sx_copy(k).wait_send()
    for k in range(1, n_y):
        far_copy(k).wait_send()
        sy_copy(k).wait_send()
    for k in range(1, n_z):
        sz_copy(k).wait_send()
    for q in range(quarters):
        core_copy(q).wait_send()
        for k in range(1, n_x):
            x_copy(q, k).wait_send()
        for k in range(1, n_y):
            y_copy(q, k).wait_send()
        for k in range(1, n_z):
            z_copies[q](k).wait_send()


def hand_out(
    feats_in, grad_in, small_ref, feats_ref, grad_ref, gwz_ref, ggz_ref, gbz_ref, gg1_ref, gb1_ref
):
    feats_ref[...] = feats_in[...]
    grad_ref[...] = grad_in[...]
    gwz_ref[0:8, :] = small_ref[0]
    rest = small_ref[1]
    gwz_ref[8:10, :] = rest[0:2]
    ggz_ref[...] = rest[2:3]
    gbz_ref[...] = rest[3:4]
    gg1_ref[...] = rest[4:5]
    gb1_ref[...] = rest[5:6]


def on_device(n_dp, n_z, audio, send, place, cot, conv_zero, conv_one, gz, bz, g1, b1):
    n_x = n_dp // (n_core * n_y)
    n_rows, n_out, width = audio.shape[1], cot.shape[1], cot.shape[2]
    n_even = n_out + tail_rows
    per_owner = 3 * width // 8 // n_dp
    n_near = n_x * n_core
    vmem = lambda *shape, dtype=F32: pltpu.VMEM(shape, dtype)
    page = lambda *shape: pltpu.VMEM((*shape, per_owner, 8, width // quarters), BF16)
    dma = lambda *shape: pltpu.SemaphoreType.DMA(shape)
    scratch = [
        vmem(40, n_rows, dtype=BF16),
        vmem(1, n_dp * slots, dtype=jnp.int32),
        vmem(1, n_rows, dtype=jnp.int32),
        vmem(10, width, dtype=BF16),
        *[vmem(1, width)] * 4,
        vmem(n_out, width, dtype=BF16),
        vmem(3 * width, width, dtype=BF16),
        vmem(n_out, width, dtype=BF16),
        vmem(n_near, n_y, 1, lanes),
        vmem(n_near, n_y, 1, lanes),
        vmem(n_y, n_near, 1, lanes),
        vmem(8, lanes),
        vmem(8, lanes),
        vmem(n_rows + 8, lanes),
        vmem(n_even, lanes, dtype=BF16),
        vmem(128, width, dtype=BF16),
        vmem(n_even, width, dtype=BF16),
        vmem(n_out, width, dtype=BF16),
        vmem(n_even, width),
        vmem(n_out, width),
        vmem(n_even, width),
        vmem(n_out, width),
        vmem(n_even, 1),
        vmem(n_out, 1),
        vmem(n_even, width),
        vmem(n_out, width, dtype=BF16),
        vmem(n_out + 32, width),
        vmem(n_even, width, dtype=BF16),
        vmem(n_even, width, dtype=BF16),
        vmem(n_even, width, dtype=BF16),
        vmem(n_out, width, dtype=BF16),
        vmem(n_out, width, dtype=BF16),
        page(quarters, n_core, n_x, n_y),
        page(quarters, n_x, n_y),
        page(quarters, n_x, n_y),
        page(quarters, n_x, n_y),
        page(quarters, n_y),
        page(quarters, n_y),
        page(n_y, n_x),
        page(n_x),
        page(n_x),
        page(quarters, n_z),
        vmem(2, 8, width),
        vmem(8, width),
        vmem(n_x, 8, width),
        vmem(n_y, 8, width),
        vmem(n_z, 8, width, dtype=BF16),
        vmem(8, width),
        dma(11),
        dma(n_near),
        dma(n_near),
        dma(n_y),
        dma(n_y),
        dma(2),
        dma(quarters),
        dma(quarters),
        dma(quarters, n_x),
        dma(quarters, n_x),
        dma(quarters, n_y),
        dma(quarters, n_y),
        dma(quarters, n_z),
        dma(quarters, n_z),
        dma(2),
        dma(n_x),
        dma(n_x),
        dma(n_y),
        dma(n_y),
        dma(n_z),
        dma(n_z),
        dma(2),
        pltpu.SemaphoreType.REGULAR((2,)),
        pltpu.SemaphoreType.REGULAR((2,)),
    ]
    row = jax.ShapeDtypeStruct((1, width), F32)
    in_vmem = pl.BlockSpec(memory_space=pltpu.VMEM)
    anywhere = pl.BlockSpec(memory_space=pl.ANY)
    feats, grad, small = pl.pallas_call(
        functools.partial(kernel, (n_dp, n_x, n_z, n_rows, n_out, width)),
        out_shape=(
            jax.ShapeDtypeStruct((n_out, width), BF16),
            jax.ShapeDtypeStruct((3 * width // n_dp, width), F32),
            jax.ShapeDtypeStruct((2, 8, width), F32),
        ),
        in_specs=[anywhere] * 10,
        out_specs=(anywhere, in_vmem, in_vmem),
        scratch_shapes=scratch,
        compiler_params=pltpu.CompilerParams(
            collective_id=0, has_side_effects=True, vmem_limit_bytes=60 * 2**20
        ),
    )(
        audio[0].T,
        send.reshape(1, -1),
        place.reshape(1, -1),
        cot[0],
        conv_zero,
        conv_one,
        gz[None],
        bz[None],
        g1[None],
        b1[None],
    )
    feats, grad, gwz, ggz, gbz, gg1, gb1 = pl.pallas_call(
        hand_out,
        out_shape=(
            jax.ShapeDtypeStruct(feats.shape, feats.dtype),
            jax.ShapeDtypeStruct(grad.shape, grad.dtype),
            jax.ShapeDtypeStruct((10, width), F32),
            row,
            row,
            row,
            row,
        ),
        in_specs=[in_vmem] * 3,
        out_specs=(in_vmem,) * 7,
        compiler_params=pltpu.CompilerParams(vmem_limit_bytes=60 * 2**20),
    )(feats, grad, small)
    return feats[None], grad, gwz, ggz[0], gbz[0], gg1[0], gb1[0]


def solution(mesh):
    placed = (
        P("dp", "seq", None),
        P("seq", "dp", None),
        P("seq", "dp", None),
        P("dp", "seq", None),
        P(),
        P(),
        P(),
        P(),
        P(),
        P(),
    )
    return jax.shard_map(
        functools.partial(on_device, mesh.shape["dp"], mesh.shape["seq"]),
        mesh=mesh,
        in_specs=placed,
        out_specs=(P("dp", "seq", None), P("dp", None), P(), P(), P(), P(), P()),
        check_vma=False,
    )
```

```python
import functools

import jax
import jax.numpy as jnp
from jax import lax
from jax.experimental import pallas as pl
from jax.experimental.pallas import tpu as pltpu
from jax.sharding import PartitionSpec as P

MESH = pl.DeviceIdType.MESH
F32 = jnp.float32
BF16 = jnp.bfloat16
norm_eps = 1e-05
n_core = 2
n_y = 8
slots = 4
group = 64
lanes = slots * group
chunk_zero = 512
chunk_one = 512
chunk_back = 256
tail_rows = 16
quarters = 4


def iota(shape, dim):
    return lax.broadcasted_iota(jnp.int32, shape, dim)


def one_hot(mask):
    return jnp.where(mask, 1.0, 0.0).astype(BF16)


def dot(a, b, dims=((1,), (0,))):
    return lax.dot_general(a, b, (dims, ((), ())), preferred_element_type=F32)


TN = ((0,), (0,))
NT = ((1,), (1,))


def norm_gelu(pre, gain, bias):
    center = pre - jnp.mean(pre, axis=-1, keepdims=True)
    spread = lax.rsqrt(jnp.mean(center * center, axis=-1, keepdims=True) + norm_eps)
    scaled = center * spread
    normed = scaled * gain + bias
    below = 0.5 + 0.5 * lax.erf(normed * 0.7071067811865476)
    act = normed * below
    slope = below + normed * (jnp.exp(-0.5 * normed * normed) * 0.3989422804014327)
    return act, scaled, spread, slope


def norm_back(upstream, gain, scaled, spread, slope):
    inner = upstream * slope
    pushed = inner * gain
    back = spread * (
        pushed
        - jnp.mean(pushed, axis=-1, keepdims=True)
        - scaled * jnp.mean(pushed * scaled, axis=-1, keepdims=True)
    )
    return back, inner * scaled, inner


def fold_rows(array):
    return jnp.sum(array.reshape(array.shape[0] // 8, 8, array.shape[1]), axis=0)


def kernel(
    sizes,
    audio_hbm,
    send_hbm,
    place_hbm,
    cot_hbm,
    wz_hbm,
    w_hbm,
    gz_hbm,
    bz_hbm,
    g1_hbm,
    b1_hbm,
    feats_hbm,
    grad_ref,
    small_full,
    audio_ref,
    send_ref,
    place_ref,
    wz_ref,
    gz_ref,
    bz_ref,
    g1_ref,
    b1_ref,
    cot_ref,
    w_ref,
    feats_ref,
    msg,
    got_msg,
    arr,
    own_row,
    rim,
    samples,
    patches,
    wz_pad,
    act_even,
    act_odd,
    scaled_even,
    scaled_odd,
    slope_even,
    slope_odd,
    spread_even,
    spread_odd,
    third,
    back_one,
    back_f32,
    back_down,
    hi_even,
    lo_even,
    hi_odd,
    lo_odd,
    parts,
    got_core,
    sum_core,
    got_x,
    sum_x,
    got_y,
    got_y_first,
    sum_y_first,
    got_x_second,
    got_z,
    small,
    small_core,
    small_x,
    small_y,
    small_z,
    small_half,
    load_sems,
    near_send,
    near_recv,
    far_send,
    far_recv,
    rim_sems,
    core_send,
    core_recv,
    x_send,
    x_recv,
    y_send,
    y_recv,
    z_send,
    z_recv,
    sc_sems,
    sx_send,
    sx_recv,
    sy_send,
    sy_recv,
    sz_send,
    sz_recv,
    sf_sems,
    y_ready,
    z_ready,
):
    n_dp, n_x, n_z, n_rows, n_out, width = sizes
    n_even = n_out + tail_rows
    me = lax.axis_index("dp")
    z = lax.axis_index("seq")
    core = lax.rem(me, n_core)
    y = lax.rem(me // n_core, n_y)
    x = me // (n_core * n_y)

    def dp_of(px, py, pc):
        return (px * n_y + py) * n_core + pc

    n_near = n_x * n_core
    near = x * n_core + core

    def near_peer(k):
        at = lax.rem(near + k, n_near)
        return at, dp_of(at // n_core, y, lax.rem(at, n_core))

    def y_peer(k):
        at = lax.rem(y + k, n_y)
        return at, dp_of(x, at, core)

    barrier = pltpu.get_barrier_semaphore()

    def greet(axis, device):
        pl.semaphore_signal(barrier, inc=1, device_id={axis: device}, device_id_type=MESH)

    y_next = sorted({1, n_y - 1})
    z_next = sorted({1, n_z - 1})
    for k in z_next:
        greet("seq", lax.rem(z + k, n_z))
    for k in y_next:
        greet("dp", y_peer(k)[1])
    for k in range(1, n_near):
        greet("dp", near_peer(k)[1])

    def rounds(count, ready, axis, device):
        for _ in range(2, count // 2 + 1):
            for side, k in enumerate((1, count - 1)):
                pl.semaphore_signal(
                    ready.at[side], inc=1, device_id={axis: device(k)}, device_id_type=MESH
                )
            yield
            for side in range(2):
                pl.semaphore_wait(ready.at[side], 1)

    y_rounds = rounds(n_y, y_ready, "dp", lambda k: y_peer(k)[1])
    z_rounds = rounds(n_z, z_ready, "seq", lambda k: lax.rem(z + k, n_z))

    def step(some_rounds):
        next(some_rounds, None)

    def load(src, dst, at):
        copy = pltpu.make_async_copy(src, dst, load_sems.at[at])
        copy.start()
        return copy

    load_message = [load(audio_hbm, audio_ref, 3), load(send_hbm, send_ref, 4)]
    load_small = [
        load(src, dst, 5 + at)
        for at, (src, dst) in enumerate(
            (
                (place_hbm, place_ref),
                (wz_hbm, wz_ref),
                (gz_hbm, gz_ref),
                (bz_hbm, bz_ref),
                (g1_hbm, g1_ref),
                (b1_hbm, b1_ref),
            )
        )
    ]
    load_w = load(w_hbm, w_ref, 0)
    load_cot = load(cot_hbm, cot_ref, 1)

    spread_lanes = one_hot(
        jnp.bitwise_and(iota((40, lanes), 1), group - 1) == iota((40, lanes), 0)
    )
    for copy in load_message:
        copy.wait()
    blocks = dot(audio_ref[...], spread_lanes, TN).astype(BF16)
    chosen = one_hot(iota((n_rows, n_dp * slots), 0) == send_ref[...])
    picked = dot(chosen, blocks, TN)
    slot_of = jnp.bitwise_and(iota((n_dp * slots, lanes), 0), slots - 1)
    lane_group = lax.shift_right_logical(iota((n_dp * slots, lanes), 1), 6)
    in_group = slot_of == lane_group
    picked = jnp.where(in_group, picked, 0.0).astype(BF16)
    bit_y = n_y.bit_length() - 1

    def of_slot(shape, dim):
        device = lax.shift_right_logical(iota(shape, dim), 2)
        at_core = jnp.bitwise_and(device, n_core - 1)
        at_y = jnp.bitwise_and(lax.shift_right_logical(device, 1), n_y - 1)
        return lax.shift_right_logical(device, 1 + bit_y) * n_core + at_core, at_y

    slot_near, slot_y = of_slot((n_dp, n_dp * slots), 1)
    gather_dest = one_hot(slot_near * n_y + slot_y == iota((n_dp, n_dp * slots), 0))
    message = dot(gather_dest, picked)
    for d in range(n_dp):
        msg[d // n_y, d % n_y] = message[d : d + 1]

    pl.semaphore_wait(barrier, n_near - 1 + len(y_next) + len(z_next))
    step(y_rounds)
    step(z_rounds)

    def near_copy(k):
        at, device = near_peer(k)
        return pltpu.make_async_remote_copy(
            src_ref=msg.at[at],
            dst_ref=got_msg.at[near],
            send_sem=near_send.at[k],
            recv_sem=near_recv.at[k],
            device_id={"dp": device},
            device_id_type=MESH,
        )

    for k in range(1, n_near):
        near_copy(k).start()
    got_msg[near] = msg[near]

    for copy in load_small:
        copy.wait()
    wz_pad[...] = jnp.zeros_like(wz_pad)
    wz_pad[0:10, :] = wz_ref[...]
    gain_zero, bias_zero = gz_ref[...], bz_ref[...]
    gain_one, bias_one = g1_ref[...], b1_ref[...]
    keep = jnp.where(z < n_z - 1, 1.0, 0.0).astype(F32)
    placed = one_hot(iota((n_dp * slots, n_rows), 0) == place_ref[...])
    slot_near, slot_y = of_slot((n_dp * slots, n_dp), 0)
    spread_slots = one_hot(slot_y * n_near + slot_near == iota((n_dp * slots, n_dp), 1))
    for _ in range(n_y):
        step(y_rounds)
    for k in range(1, n_near):
        near_copy(k).wait_recv()

    def far_copy(k):
        at, device = y_peer(k)
        return pltpu.make_async_remote_copy(
            src_ref=got_msg.at[:, at],
            dst_ref=arr.at[y],
            send_sem=far_send.at[k],
            recv_sem=far_recv.at[k],
            device_id={"dp": device},
            device_id_type=MESH,
        )

    order_y = sorted(range(1, n_y), key=lambda k: -min(k, n_y - k))
    order_z = sorted(range(1, n_z), key=lambda k: -min(k, n_z - k))
    for k in order_y:
        far_copy(k).start()
    arr[y] = got_msg[:, y]
    lane_in, lane_out = iota((lanes, lanes), 0), iota((lanes, lanes), 1)
    sample_in = jnp.bitwise_and(lane_in, group - 1)
    sample_out = jnp.bitwise_and(lane_out, group - 1)
    fold_here = one_hot((sample_in == sample_out) & (sample_out < 40))
    fold_next = one_hot((sample_in + 40 == sample_out) & (sample_out < 45))
    row_id = iota((n_out, n_rows), 0)
    widen = one_hot(lax.shift_right_logical(row_id, 2) == iota((n_out, n_rows), 1))
    phase = jnp.bitwise_and(iota((n_out, lanes), 0), 3)
    own_phase = phase == lax.shift_right_logical(iota((n_out, lanes), 1), 6)
    tap = sample_in - 10 * lax.shift_right_logical(lane_in, 6)
    wanted = jnp.where(lane_out < 128, lane_out, lane_out - 128 + 5)
    limit = jnp.where(lane_out < 128, 10, 15)
    to_patch = one_hot((tap == wanted) & (wanted < limit))
    edge_from = jnp.where(lane_out < 128, lane_out, lane_out - 133)
    edge_limit = jnp.where(lane_out < 128, 10, 5)
    to_edge = one_hot((sample_in == edge_from) & (edge_from < edge_limit))

    for k in range(1, n_y):
        far_copy(k).wait_recv()

    received = jnp.concatenate(
        [arr[s // n_near, s % n_near] for s in range(n_dp)], axis=0
    ).astype(BF16)
    by_slot = dot(spread_slots, received)
    by_slot = jnp.where(in_group, by_slot, 0.0).astype(BF16)
    ordered = dot(placed, by_slot, TN)
    own_row[...] = dot(ordered[0:8].astype(BF16), to_edge)
    rim_copy = pltpu.make_async_remote_copy(
        src_ref=own_row,
        dst_ref=rim,
        send_sem=rim_sems.at[0],
        recv_sem=rim_sems.at[1],
        device_id={"seq": lax.rem(z + n_z - 1, n_z)},
        device_id_type=MESH,
    )
    rim_copy.start()
    samples[0:n_rows, :] = ordered
    samples[n_rows : n_rows + 8, :] = jnp.zeros((8, lanes), F32)
    wide = dot(samples[0:n_rows, :].astype(BF16), fold_here) + dot(
        samples[1 : n_rows + 1, :].astype(BF16), fold_next
    )
    rows = dot(widen, wide.astype(BF16))
    rows = jnp.where(own_phase, rows, 0.0).astype(BF16)
    patches[0:n_out, :] = dot(rows, to_patch).astype(BF16)

    step(z_rounds)
    def forward_even(r, n):
        pre = dot(patches[pl.ds(r, n), 0:128], wz_pad[...])
        act, scaled, spread, slope = norm_gelu(pre, gain_zero, bias_zero)
        scaled_even[pl.ds(r, n), :] = scaled
        slope_even[pl.ds(r, n), :] = slope
        spread_even[pl.ds(r, n), :] = spread
        return act

    def forward_odd(r, n):
        pre = dot(patches[pl.ds(r, n), 128:256], wz_pad[...])
        act, scaled, spread, slope = norm_gelu(pre, gain_zero, bias_zero)
        act_odd[pl.ds(r, n), :] = act.astype(BF16)
        scaled_odd[pl.ds(r, n), :] = scaled
        slope_odd[pl.ds(r, n), :] = slope
        spread_odd[pl.ds(r, n), :] = spread

    def forward_zero(i, carry):
        r = pl.multiple_of(i * chunk_zero, chunk_zero)
        act_even[pl.ds(r, chunk_zero), :] = forward_even(r, chunk_zero).astype(BF16)
        forward_odd(r, chunk_zero)
        return carry

    lax.fori_loop(0, n_out // chunk_zero, forward_zero, 0)

    step(z_rounds)
    rim_copy.wait_recv()
    edge = rim[0:1, :] * keep
    tail_id = iota((tail_rows, 128), 0)
    last = pl.ds(n_out - tail_rows, tail_rows)
    patches[last, 128:256] = (
        patches[last, 128:256].astype(F32)
        + jnp.where(tail_id == tail_rows - 1, edge[:, 128:256], 0.0)
    ).astype(BF16)
    patches[n_out:n_even, 0:128] = jnp.where(tail_id == 0, edge[:, 0:128], 0.0).astype(BF16)
    forward_odd(n_out - tail_rows, tail_rows)
    act_even[n_out:n_even, :] = (forward_even(n_out, tail_rows) * keep).astype(BF16)
    load_w.wait()

    step(z_rounds)
    third[...] = dot(act_even[...], w_ref[2 * width : 3 * width, :])
    for r in range(0, n_out, 64):
        third[r : r + 64, :] = third[r + 1 : r + 65, :]
    load_cot.wait()

    def layer_one(i, carry):
        sum_gain, sum_bias = carry
        r = pl.multiple_of(i * chunk_one, chunk_one)
        here = pl.ds(r, chunk_one)
        pre = (
            dot(act_even[here, :], w_ref[0:width, :])
            + dot(act_odd[here, :], w_ref[width : 2 * width, :])
            + third[here, :]
        )
        act, scaled, spread, slope = norm_gelu(pre, gain_one, bias_one)
        feats_ref[here, :] = act.astype(BF16)
        back, gain_term, bias_term = norm_back(
            cot_ref[here, :].astype(F32), gain_one, scaled, spread, slope
        )
        back = back.astype(BF16)
        back_one[here, :] = back
        back_f32[pl.ds(r + 8, chunk_one), :] = back.astype(F32)
        return (sum_gain + fold_rows(gain_term), sum_bias + fold_rows(bias_term))

    zero_sum = jnp.zeros((8, width), F32)
    back_f32[0:8, :] = jnp.zeros((8, width), F32)
    back_f32[n_out + 8 :, :] = jnp.zeros((back_f32.shape[0] - n_out - 8, width), F32)
    sum_gain_one, sum_bias_one = lax.fori_loop(
        0, n_out // chunk_one, layer_one, (zero_sum, zero_sum)
    )
    step(z_rounds)
    back_down[...] = back_f32[7 : 7 + n_even, :].astype(BF16)

    keep_feats = pltpu.make_async_copy(feats_ref, feats_hbm, load_sems.at[2])
    keep_feats.start()

    per_owner = 3 * width // 8 // n_dp
    cols = width // quarters
    partner = dp_of(x, y, 1 - core)

    def keep_pages(first_page, quarter, value):
        for i in range(width // 8):
            page = first_page + i
            d, j = page // per_owner, page % per_owner
            px, py, pc = d // (n_core * n_y), (d // n_core) % n_y, d % n_core
            for q in range(2):
                parts[quarter + q, pc, px, py, j] = value[
                    8 * i : 8 * i + 8, q * cols : (q + 1) * cols
                ].astype(BF16)

    def core_copy(q):
        return pltpu.make_async_remote_copy(
            src_ref=parts.at[q, 1 - core],
            dst_ref=got_core.at[q],
            send_sem=core_send.at[q],
            recv_sem=core_recv.at[q],
            device_id={"dp": partner},
            device_id_type=MESH,
        )

    for q in range(0, quarters, 2):
        here = slice(q * cols, (q + 2) * cols)
        keep_pages(0, q, dot(act_even[0:n_out, :], back_one[:, here], TN))
        keep_pages(width // 8, q, dot(act_odd[...], back_one[:, here], TN))
        keep_pages(2 * width // 8, q, dot(act_even[...], back_down[:, here], TN))
        core_copy(q).start()
        core_copy(q + 1).start()

    def back_zero(r, n, upstream, scaled_ref, slope_ref, spread_ref, hi_ref, lo_ref):
        here = pl.ds(r, n)
        back, gain_term, bias_term = norm_back(
            upstream, gain_zero, scaled_ref[here, :], spread_ref[here, :], slope_ref[here, :]
        )
        hi = back.astype(BF16)
        hi_ref[here, :] = hi
        lo_ref[here, :] = (back - hi.astype(F32)).astype(BF16)
        return fold_rows(gain_term), fold_rows(bias_term)

    def back_even(i, carry):
        r = pl.multiple_of(i * chunk_back, chunk_back)
        here = pl.ds(r, chunk_back)
        upstream = dot(back_one[here, :], w_ref[0:width, :], NT) + dot(
            back_down[here, :], w_ref[2 * width : 3 * width, :], NT
        )
        terms = back_zero(
            r, chunk_back, upstream, scaled_even, slope_even, spread_even, hi_even, lo_even
        )
        return (carry[0] + terms[0], carry[1] + terms[1])

    def back_odd(i, carry):
        r = pl.multiple_of(i * chunk_back, chunk_back)
        here = pl.ds(r, chunk_back)
        upstream = dot(back_one[here, :], w_ref[width : 2 * width, :], NT)
        terms = back_zero(
            r, chunk_back, upstream, scaled_odd, slope_odd, spread_odd, hi_odd, lo_odd
        )
        return (carry[0] + terms[0], carry[1] + terms[1])

    order_x = sorted(range(1, n_x), key=lambda k: -min(k, n_x - k))

    def x_peer(k):
        at = lax.rem(x + k, n_x)
        return at, dp_of(at, y, core)

    def send(src, dst, send_sem, recv_sem, axis, device):
        return pltpu.make_async_remote_copy(
            src_ref=src,
            dst_ref=dst,
            send_sem=send_sem,
            recv_sem=recv_sem,
            device_id={axis: device},
            device_id_type=MESH,
        )

    def x_copy(q, k):
        at, device = x_peer(k)
        src, dst = (
            (sum_y_first.at[at], got_x_second.at[k])
            if q == 0
            else (sum_core.at[q, at], got_x.at[q, k])
        )
        return send(src, dst, x_send.at[q, k], x_recv.at[q, k], "dp", device)

    def y_copy(q, k):
        at, device = y_peer(k)
        src, dst = (
            (sum_core.at[0, :, at], got_y_first.at[k])
            if q == 0
            else (sum_x.at[q, at], got_y.at[q, k])
        )
        return send(src, dst, y_send.at[q, k], y_recv.at[q, k], "dp", device)

    def pair_sum(q):
        core_copy(q).wait_recv()

        def add_core(i, carry):
            total = parts[q, core, i].astype(F32) + got_core[q, i].astype(F32)
            sum_core[q, i] = total.astype(BF16)
            return carry

        lax.fori_loop(0, n_x, add_core, 0)
        if q == 0:
            for k in order_y:
                y_copy(0, k).start()
        else:
            for k in order_x:
                x_copy(q, k).start()

    sums = back_even(0, (zero_sum, zero_sum))
    pair_sum(0)
    pair_sum(1)
    n_chunks = n_out // chunk_back
    if n_chunks > 1:
        sums = back_even(1, sums)
    pair_sum(2)
    pair_sum(3)
    for i in range(2, n_chunks):
        sums = back_even(i, sums)
    upstream = (
        dot(back_down[n_out:n_even, :], w_ref[2 * width : 3 * width, :], NT) * keep
    )
    terms = back_zero(
        n_out, tail_rows, upstream, scaled_even, slope_even, spread_even, hi_even, lo_even
    )
    sums = (sums[0] + terms[0], sums[1] + terms[1])
    sums = lax.fori_loop(0, n_chunks, back_odd, sums)

    grad_wz = (
        dot(patches[:, 0:128], hi_even[...], TN)
        + dot(patches[:, 0:128], lo_even[...], TN)
        + dot(patches[0:n_out, 128:256], hi_odd[...], TN)
        + dot(patches[0:n_out, 128:256], lo_odd[...], TN)
    )

    def row_sum(array):
        return jnp.sum(array, axis=0, keepdims=True)

    small[0, :, :] = grad_wz[0:8]
    small[1, 0:2, :] = grad_wz[8:10]
    small[1, 2:3, :] = row_sum(sums[0])
    small[1, 3:4, :] = row_sum(sums[1])
    small[1, 4:5, :] = row_sum(sum_gain_one)
    small[1, 5:6, :] = row_sum(sum_bias_one)
    small[1, 6:8, :] = jnp.zeros((2, width), F32)
    small_core_copy = pltpu.make_async_remote_copy(
        src_ref=small.at[1 - core],
        dst_ref=small_core,
        send_sem=sc_sems.at[0],
        recv_sem=sc_sems.at[1],
        device_id={"dp": partner},
        device_id_type=MESH,
    )
    small_core_copy.start()

    def share(buffer, at, sends, recvs, axis, device):
        def copy(k):
            return pltpu.make_async_remote_copy(
                src_ref=buffer.at[at],
                dst_ref=buffer.at[at],
                send_sem=sends.at[k],
                recv_sem=recvs.at[k],
                device_id={axis: device(k)},
                device_id_type=MESH,
            )

        return copy

    sx_copy = share(small_x, x, sx_send, sx_recv, "dp", lambda k: x_peer(k)[1])
    sy_copy = share(small_y, y, sy_send, sy_recv, "dp", lambda k: y_peer(k)[1])
    sz_copy = share(small_z, z, sz_send, sz_recv, "seq", lambda k: lax.rem(z + k, n_z))
    z_copies = [
        share(
            got_z.at[q], z, z_send.at[q], z_recv.at[q], "seq", lambda k: lax.rem(z + k, n_z)
        )
        for q in range(quarters)
    ]

    def total_of(buffer, count):
        total = buffer[0].astype(F32)
        for k in range(1, count):
            total = total + buffer[k].astype(F32)
        return total

    def plus_got(total, buffer, count):
        total = total.astype(F32)
        for k in range(1, count):
            total = total + buffer[k].astype(F32)
        return total.astype(BF16)

    def got_all(copy, count):
        for k in range(1, count):
            copy(k).wait_recv()

    def along_y(q):
        got_all(functools.partial(x_copy, q), n_x)
        sum_x[q] = plus_got(sum_core[q, x], got_x.at[q], n_x)
        for k in order_y:
            y_copy(q, k).start()

    def along_z(q):
        if q == 0:
            got_all(functools.partial(x_copy, 0), n_x)
            got_z[0, z] = plus_got(sum_y_first[x], got_x_second, n_x)
        else:
            got_all(functools.partial(y_copy, q), n_y)
            got_z[q, z] = plus_got(sum_x[q, y], got_y.at[q], n_y)
        for k in order_z:
            z_copies[q](k).start()

    def finish(q):
        got_all(z_copies[q], n_z)
        total = total_of(got_z.at[q], n_z)
        for j in range(per_owner):
            grad_ref[8 * j : 8 * j + 8, q * cols : (q + 1) * cols] = total[j]

    for _ in range(n_z):
        step(z_rounds)
    along_y(1)
    small_core_copy.wait_recv()
    small_z[z] = (small[core] + small_core[...]).astype(BF16)
    for k in order_z:
        sz_copy(k).start()
    along_y(2)
    got_all(functools.partial(y_copy, 0), n_y)
    sum_y_first[...] = plus_got(sum_core[0, :, y], got_y_first, n_y)
    for k in order_x:
        x_copy(0, k).start()
    along_y(3)
    along_z(1)
    along_z(0)
    got_all(sz_copy, n_z)
    small_x[x] = total_of(small_z, n_z)
    for k in order_x:
        sx_copy(k).start()
    along_z(2)
    got_all(sx_copy, n_x)
    small_y[y] = total_of(small_x, n_x)
    for k in order_y:
        sy_copy(k).start()
    along_z(3)
    finish(1)
    finish(0)
    got_all(sy_copy, n_y)
    total = total_of(small_y, n_y)
    small_half[...] = total
    full_copy = send(
        small_half, small_full.at[core], sf_sems.at[0], sf_sems.at[1], "dp", partner
    )
    full_copy.start()
    small_full[core] = total
    finish(2)
    finish(3)
    full_copy.wait_recv()

    keep_feats.wait()
    rim_copy.wait_send()
    small_core_copy.wait_send()
    full_copy.wait_send()
    for k in range(1, n_near):
        near_copy(k).wait_send()
    for k in range(1, n_x):
        sx_copy(k).wait_send()
    for k in range(1, n_y):
        far_copy(k).wait_send()
        sy_copy(k).wait_send()
    for k in range(1, n_z):
        sz_copy(k).wait_send()
    for q in range(quarters):
        core_copy(q).wait_send()
        for k in range(1, n_x):
            x_copy(q, k).wait_send()
        for k in range(1, n_y):
            y_copy(q, k).wait_send()
        for k in range(1, n_z):
            z_copies[q](k).wait_send()


def hand_out(
    feats_in, grad_in, small_ref, feats_ref, grad_ref, gwz_ref, ggz_ref, gbz_ref, gg1_ref, gb1_ref
):
    feats_ref[...] = feats_in[...]
    grad_ref[...] = grad_in[...]
    gwz_ref[0:8, :] = small_ref[0]
    rest = small_ref[1]
    gwz_ref[8:10, :] = rest[0:2]
    ggz_ref[...] = rest[2:3]
    gbz_ref[...] = rest[3:4]
    gg1_ref[...] = rest[4:5]
    gb1_ref[...] = rest[5:6]


def on_device(n_dp, n_z, audio, send, place, cot, conv_zero, conv_one, gz, bz, g1, b1):
    n_x = n_dp // (n_core * n_y)
    n_rows, n_out, width = audio.shape[1], cot.shape[1], cot.shape[2]
    n_even = n_out + tail_rows
    per_owner = 3 * width // 8 // n_dp
    n_near = n_x * n_core
    vmem = lambda *shape, dtype=F32: pltpu.VMEM(shape, dtype)
    page = lambda *shape: pltpu.VMEM((*shape, per_owner, 8, width // quarters), BF16)
    dma = lambda *shape: pltpu.SemaphoreType.DMA(shape)
    scratch = [
        vmem(40, n_rows, dtype=BF16),
        vmem(1, n_dp * slots, dtype=jnp.int32),
        vmem(1, n_rows, dtype=jnp.int32),
        vmem(10, width, dtype=BF16),
        *[vmem(1, width)] * 4,
        vmem(n_out, width, dtype=BF16),
        vmem(3 * width, width, dtype=BF16),
        vmem(n_out, width, dtype=BF16),
        vmem(n_near, n_y, 1, lanes),
        vmem(n_near, n_y, 1, lanes),
        vmem(n_y, n_near, 1, lanes),
        vmem(8, lanes),
        vmem(8, lanes),
        vmem(n_rows + 8, lanes),
        vmem(n_even, lanes, dtype=BF16),
        vmem(128, width, dtype=BF16),
        vmem(n_even, width, dtype=BF16),
        vmem(n_out, width, dtype=BF16),
        vmem(n_even, width),
        vmem(n_out, width),
        vmem(n_even, width),
        vmem(n_out, width),
        vmem(n_even, 1),
        vmem(n_out, 1),
        vmem(n_even, width),
        vmem(n_out, width, dtype=BF16),
        vmem(n_out + 32, width),
        vmem(n_even, width, dtype=BF16),
        vmem(n_even, width, dtype=BF16),
        vmem(n_even, width, dtype=BF16),
        vmem(n_out, width, dtype=BF16),
        vmem(n_out, width, dtype=BF16),
        page(quarters, n_core, n_x, n_y),
        page(quarters, n_x, n_y),
        page(quarters, n_x, n_y),
        page(quarters, n_x, n_y),
        page(quarters, n_y),
        page(quarters, n_y),
        page(n_y, n_x),
        page(n_x),
        page(n_x),
        page(quarters, n_z),
        vmem(2, 8, width),
        vmem(8, width),
        vmem(n_x, 8, width),
        vmem(n_y, 8, width),
        vmem(n_z, 8, width, dtype=BF16),
        vmem(8, width),
        dma(11),
        dma(n_near),
        dma(n_near),
        dma(n_y),
        dma(n_y),
        dma(2),
        dma(quarters),
        dma(quarters),
        dma(quarters, n_x),
        dma(quarters, n_x),
        dma(quarters, n_y),
        dma(quarters, n_y),
        dma(quarters, n_z),
        dma(quarters, n_z),
        dma(2),
        dma(n_x),
        dma(n_x),
        dma(n_y),
        dma(n_y),
        dma(n_z),
        dma(n_z),
        dma(2),
        pltpu.SemaphoreType.REGULAR((2,)),
        pltpu.SemaphoreType.REGULAR((2,)),
    ]
    row = jax.ShapeDtypeStruct((1, width), F32)
    in_vmem = pl.BlockSpec(memory_space=pltpu.VMEM)
    anywhere = pl.BlockSpec(memory_space=pl.ANY)
    feats, grad, small = pl.pallas_call(
        functools.partial(kernel, (n_dp, n_x, n_z, n_rows, n_out, width)),
        out_shape=(
            jax.ShapeDtypeStruct((n_out, width), BF16),
            jax.ShapeDtypeStruct((3 * width // n_dp, width), F32),
            jax.ShapeDtypeStruct((2, 8, width), F32),
        ),
        in_specs=[anywhere] * 10,
        out_specs=(anywhere, in_vmem, in_vmem),
        scratch_shapes=scratch,
        compiler_params=pltpu.CompilerParams(
            collective_id=0, has_side_effects=True, vmem_limit_bytes=60 * 2**20
        ),
    )(
        audio[0].T,
        send.reshape(1, -1),
        place.reshape(1, -1),
        cot[0],
        conv_zero,
        conv_one,
        gz[None],
        bz[None],
        g1[None],
        b1[None],
    )
    feats, grad, gwz, ggz, gbz, gg1, gb1 = pl.pallas_call(
        hand_out,
        out_shape=(
            jax.ShapeDtypeStruct(feats.shape, feats.dtype),
            jax.ShapeDtypeStruct(grad.shape, grad.dtype),
            jax.ShapeDtypeStruct((10, width), F32),
            row,
            row,
            row,
            row,
        ),
        in_specs=[in_vmem] * 3,
        out_specs=(in_vmem,) * 7,
        compiler_params=pltpu.CompilerParams(vmem_limit_bytes=60 * 2**20),
    )(feats, grad, small)
    return feats[None], grad, gwz, ggz[0], gbz[0], gg1[0], gb1[0]


def solution(mesh):
    placed = (
        P("dp", "seq", None),
        P("seq", "dp", None),
        P("seq", "dp", None),
        P("dp", "seq", None),
        P(),
        P(),
        P(),
        P(),
        P(),
        P(),
    )
    return jax.shard_map(
        functools.partial(on_device, mesh.shape["dp"], mesh.shape["seq"]),
        mesh=mesh,
        in_specs=placed,
        out_specs=(P("dp", "seq", None), P("dp", None), P(), P(), P(), P(), P()),
        check_vma=False,
    )
```
